512 devices in a mesh: stat: 16 (over z, core), tile: 32 (over x, y).
Axes of the slice: x: 4, y: 8, z: 8, core: 2. Of those that a mesh axis runs over, the one named last changes fastest.
Arguments:
- visibilities: float32 [16384, 8, 256], P(('stat', 'tile')), may hold values from -6 to 6
- weights: float32 [16384, 256], P(('stat', 'tile')), may hold values from 0.2 to 2
- uv_coords: float32 [16384, 2, 16], P(('stat', 'tile')), may hold values from -8 to 8
- freq_ratio: float32 [16], replicated, may hold values from 0.8 to 1.25
- screens: bfloat16 [512, 2, 1024], P('stat'), may hold values from -6 to 6
- stations: int32 [16384, 2], P(('stat', 'tile')), may hold values from 0 to 511
- offsets: int32 [16384, 2], P(('stat', 'tile')), may hold values from 0 to 224
- tile_ids: int32 [16384, 1], P(('stat', 'tile')), may hold values from 0 to 31; in each aligned block of 32 rows (0 to 31, 32 to 63, ...) at most 2 rows name the same one
Outputs:
- uv_grid: float32 [32, 8, 256, 256], P('tile', None, 'stat')
The draws below stay inside these ranges and needn't reach their ends.
Inputs may be any that keep to these rules, and one draw needn't show every extreme that they name: `tile_ids`: among the 32 rows of one device at most 2 name the same tile, and in every draw some device has exactly 2 rows naming one tile.
All inputs are finite; a program needn't handle non-finite values.
Results may differ from the reference program's by a relative error of at most 0.012.
Values may be sent and summed in bfloat16 or wider, within the bound.
No kernel may reach another device: no remote copies, remote signals or barrier semaphores. Data moves between devices by JAX's collectives and lax.ppermute only.
A program may use at most 64 MiB of HBM per device.

```python
import math
import jax
import jax.numpy as jnp
import numpy as np
from jax import lax

STATIONS = 512
CHANNELS = 16
SUB = 32
TS = 256
T_BLK = 16
SG_DEV = 32
K = 256
NTILES = 32
CAP = 2
SUBGRIDS = 16384


def place_ends(entries, stream_key, least, high):
    extent = entries.shape
    index_at = [jax.random.randint(jax.random.fold_in(stream_key, axis), (), 0, extent[axis]) for axis in range(len(extent))]
    entries = entries.at[tuple(index_at)].set(least)
    longest = extent.index(max(extent))
    index_at[longest] = (index_at[longest] + 1) % extent[longest]
    return entries.at[tuple(index_at)].set(high)


def block_levels(key, dims, split, smallest, high):
    def one(dim, blocks):
        draws = jax.random.uniform(jax.random.fold_in(jax.random.fold_in(key, 6), dim), (blocks,), jnp.float32, smallest / len(split), high / len(split))
        return jnp.repeat(jnp.exp(draws), dims[dim] // blocks).reshape((-1,) + (1,) * (len(dims) - dim - 1))

    gain = one(*split[0])
    for cut in split[1:]:
        gain = gain * one(*cut)
    return gain


def routed_block(stream_key, own, number, rows, number_of, top, limit, skew):
    ranking = jax.random.permutation(stream_key, number_of)
    crowded, usual = portions_of(number_of, rows * top, limit, skew, True), portions_of(number_of, rows * top, limit, skew, False)
    places = jnp.arange(number_of)

    def named(tallies, rotation):
        used = int((tallies > 0).sum())
        fixed = max(1, used // 4)
        moved = fixed + (places - fixed + rotation * (used - fixed)) % max(1, number_of - fixed)
        return jnp.zeros((number_of,), jnp.int32).at[ranking[jnp.where(places < fixed, places, moved)]].set(jnp.asarray(tallies, jnp.int32))

    tallies = jnp.where(number % 4 == 0, named(crowded, number // 4), named(usual, number - number // 4 - 1))
    mixed = jax.random.permutation(jax.random.fold_in(own, 3), number_of)
    donor, taker = mixed[0:number_of // 2 * 2:2], mixed[1:number_of // 2 * 2:2]
    slack = jnp.minimum(tallies[donor] - 1, limit - tallies[taker]) // 2
    slack = jnp.where((donor == ranking[0]) | (taker == ranking[0]) | (tallies[taker] == 0), 0, jnp.maximum(slack, 0))
    moved = jax.random.randint(jax.random.fold_in(own, 4), (number_of // 2,), 0, 1 << 20) % (slack + 1)
    tallies = tallies.at[donor].add(-moved).at[taker].add(moved)
    members = jnp.searchsorted(jnp.cumsum(tallies), jnp.arange(rows * top), side="right").astype(jnp.int32)
    grid = members.reshape(top, rows).T
    grid = grid[jax.random.permutation(jax.random.fold_in(own, 1), rows)]
    rotation = jax.random.randint(jax.random.fold_in(own, 2), (rows, 1), 0, top)
    return jnp.take_along_axis(grid, (jnp.arange(top)[None, :] + rotation) % top, axis=1)


def portions_of(count, total, most, skew, full):
    portions = [(1 << 20) // math.isqrt(rank ** skew) + 1 for rank in range(1, count + 1)]
    largest = most if full else min(most, max(-(-total // count), total * portions[0] // sum(portions)))
    least = 1 if total - largest >= count - 1 else 0
    given, spare = [largest] + [least] * (count - 1), total - largest - least * (count - 1)
    while spare > 0:
        candidates = [i for i in range(1, count) if given[i] < largest] or [i for i in range(1, count) if given[i] < most]
        whole, remaining = sum([portions[i] for i in candidates]), spare
        for i in candidates:
            extra = min(most - given[i], max(1, remaining * portions[i] // whole), spare)
            given[i] = given[i] + extra
            spare = spare - extra
    return np.array(given)


def noise(stream_key, dims, deviation, reach, split=(), kind=jnp.bfloat16):
    level = block_levels(stream_key, dims, split, -0.22, 0.18) if split else 1.0
    drawn = jax.random.normal(stream_key, dims, jnp.float32) * deviation * level
    return jnp.minimum(jnp.maximum(drawn, -reach), reach).astype(kind)


def setup_inputs(seed: int = 0) -> dict:
    key_list = jax.random.split(jax.random.key(seed), 9)
    visibilities = noise(key_list[0], (SUBGRIDS, 8, K), 1.0, 6.0, ((0, 512),), jnp.float32)
    weights = jnp.clip(jnp.exp(math.log(2.0) - 2.3025851 * jax.random.uniform(key_list[1], (SUBGRIDS, K), jnp.float32) ** block_levels(key_list[1], (SUBGRIDS, K), ((0, 512),), -0.2, 0.2)), 0.2, 2.0)
    uv_coords = jnp.clip(jax.random.uniform(key_list[2], (SUBGRIDS, 2, T_BLK), jnp.float32, -8.0, 8.0) * block_levels(key_list[2], (SUBGRIDS, 2, T_BLK), ((0, 512),), -0.4, 0.0), -8.0, 8.0)
    freq_ratio = jnp.clip(jnp.exp(jax.random.uniform(key_list[3], (CHANNELS,), jnp.float32, math.log(0.8), math.log(1.25))), 0.8, 1.25)
    screens = noise(key_list[4], (STATIONS, 2, SUB * SUB), 1.0, 6.0, ((0, 16),))
    stations = place_ends(jax.random.randint(key_list[5], (SUBGRIDS, 2), 0, STATIONS), jax.random.fold_in(key_list[5], 1), 0, STATIONS - 1).astype(jnp.int32)
    offsets = place_ends(jax.random.randint(key_list[6], (SUBGRIDS, 2), 0, TS - SUB + 1), jax.random.fold_in(key_list[6], 1), 0, TS - SUB).astype(jnp.int32)
    tile_ids_keys = jax.random.split(jax.random.fold_in(key_list[7], 1), SUBGRIDS // SG_DEV)
    tile_ids_turns = jax.random.permutation(jax.random.fold_in(key_list[7], 3), SUBGRIDS // SG_DEV)
    tile_ids = jax.vmap(lambda own, number: routed_block(jax.random.fold_in(key_list[7], 2), own, number, SG_DEV, NTILES, 1, CAP, 2))(tile_ids_keys, tile_ids_turns).reshape((SUBGRIDS, 1))
    return {"visibilities": visibilities, "weights": weights, "uv_coords": uv_coords, "freq_ratio": freq_ratio, "screens": screens, "stations": stations, "offsets": offsets, "tile_ids": tile_ids}


TWO_PI = 2.0 * math.pi


def centered(side):
    return jnp.arange(side, dtype=jnp.float32) - jnp.float32(side // 2)


def dft_operands(wvis_block, coord_block, freq_ratio):
    count_here = wvis_block.shape[0]
    delta_u = (coord_block[:, 0, :, None] * freq_ratio[None, None, :]).reshape(count_here, K)
    delta_v = (coord_block[:, 1, :, None] * freq_ratio[None, None, :]).reshape(count_here, K)
    offsets_axis = centered(SUB)
    phase_u = (TWO_PI / SUB) * delta_u[:, :, None] * offsets_axis[None, None, :]
    phase_v = (TWO_PI / SUB) * delta_v[:, :, None] * offsets_axis[None, None, :]
    left_table = jnp.concatenate([jnp.cos(phase_u), jnp.sin(phase_u)], axis=2).astype(jnp.bfloat16)
    wvis = wvis_block.astype(jnp.float32)
    wvis_re = jnp.transpose(wvis[:, :4, :], (0, 2, 1))
    wvis_im = jnp.transpose(wvis[:, 4:, :], (0, 2, 1))
    cos_v = jnp.cos(phase_v)[:, :, None, :]
    sin_v = jnp.sin(phase_v)[:, :, None, :]
    table_re = wvis_re[..., None] * cos_v - wvis_im[..., None] * sin_v
    table_im = wvis_re[..., None] * sin_v + wvis_im[..., None] * cos_v
    right_table = jnp.concatenate([table_re, table_im], axis=2).reshape(count_here, K, 8 * SUB).astype(jnp.bfloat16)
    return left_table, right_table


def finish_subgrids(product, station_block, screens):
    count_here = product.shape[0]
    parts = product.reshape(count_here, 2, SUB, 2, 4, SUB)
    real_part = jnp.transpose(parts[:, 0, :, 0] - parts[:, 1, :, 1], (0, 2, 1, 3)) / K
    imag_part = jnp.transpose(parts[:, 0, :, 1] + parts[:, 1, :, 0], (0, 2, 1, 3)) / K
    screen_p = screens[station_block[:, 0]].astype(jnp.float32)
    screen_q = screens[station_block[:, 1]].astype(jnp.float32)
    gain_re = (screen_p[:, 0] * screen_q[:, 0] + screen_p[:, 1] * screen_q[:, 1]).reshape(count_here, 1, SUB, SUB)
    gain_im = (screen_p[:, 0] * screen_q[:, 1] - screen_p[:, 1] * screen_q[:, 0]).reshape(count_here, 1, SUB, SUB)
    taper_1d = jnp.sin(math.pi * (jnp.arange(SUB, dtype=jnp.float32) + 0.5) / SUB)
    taper_2d = taper_1d[:, None] * taper_1d[None, :]
    corr_re = (gain_re * real_part - gain_im * imag_part) * taper_2d
    corr_im = (gain_re * imag_part + gain_im * real_part) * taper_2d
    offsets_axis = centered(SUB)
    dft_angle = (-TWO_PI / SUB) * offsets_axis[:, None] * offsets_axis[None, :]
    cos_table = jnp.cos(dft_angle)
    sin_table = jnp.sin(dft_angle)
    highest = lax.Precision.HIGHEST
    half_re = jnp.einsum('ul,splm->spum', cos_table, corr_re, precision=highest) - jnp.einsum('ul,splm->spum', sin_table, corr_im, precision=highest)
    half_im = jnp.einsum('ul,splm->spum', cos_table, corr_im, precision=highest) + jnp.einsum('ul,splm->spum', sin_table, corr_re, precision=highest)
    full_re = jnp.einsum('spum,vm->spuv', half_re, cos_table, precision=highest) - jnp.einsum('spum,vm->spuv', half_im, sin_table, precision=highest)
    full_im = jnp.einsum('spum,vm->spuv', half_re, sin_table, precision=highest) + jnp.einsum('spum,vm->spuv', half_im, cos_table, precision=highest)
    return (jnp.concatenate([full_re, full_im], axis=1) / SUB).astype(jnp.bfloat16)


def reference(visibilities, weights, uv_coords, freq_ratio, screens, stations, offsets, tile_ids):
    subgrid_total = visibilities.shape[0]
    block_size = math.gcd(subgrid_total, 512)
    block_count = subgrid_total // block_size
    numbers = lax.ScatterDimensionNumbers(update_window_dims=(1, 2, 3), inserted_window_dims=(0,), scatter_dims_to_operand_dims=(0, 2, 3))

    def accumulate(uv_grid, blocked):
        vis_block, weight_block, coord_block, station_block, corner_block, tile_block = blocked
        weighted = (weight_block[:, None, :] * vis_block).astype(jnp.bfloat16)
        left_table, right_table = dft_operands(weighted, coord_block, freq_ratio)
        product = jnp.einsum('skl,skn->sln', left_table.astype(jnp.float32), right_table.astype(jnp.float32))
        subgrid = finish_subgrids(product, station_block, screens)
        corner_idx = jnp.concatenate([tile_block, corner_block], axis=1).astype(jnp.int32)
        return lax.scatter_add(uv_grid, corner_idx, subgrid.astype(jnp.float32), numbers), None

    arrays = (visibilities, weights, uv_coords, stations, offsets, tile_ids)
    blocked = tuple(array_in.reshape((block_count, block_size) + array_in.shape[1:]) for array_in in arrays)
    empty_grid = jnp.zeros((NTILES, 8, TS, TS), jnp.float32)
    uv_grid, unused = lax.scan(accumulate, empty_grid, blocked)
    return uv_grid
```

```python
import functools
import math

import jax
import jax.numpy as jnp
import numpy as np
from jax import lax
from jax.experimental import pallas as pl
from jax.experimental.pallas import tpu as pltpu
from jax.sharding import PartitionSpec as P

SUB = 32
TS = 256
K = 256
SLOTS = 64
PEERS = 32
F32 = jnp.float32
BF16 = jnp.bfloat16

ROW_L = np.array([4 * (r % 8) + r // 8 for r in range(SUB)])
LANE = np.arange(256)
LANE_I = LANE % 16
LANE_P = (LANE // 16) % 4
LANE_RI = (LANE // 64) % 2
LANE_M = np.where(LANE < 128, 16 + LANE_I, 15 - LANE_I)


def spread_tables():
    out = np.zeros((4, 256, 256), np.float32)
    for part in range(3):
        for t in range(16):
            out[0, part * 32 + t, t * 16 : (t + 1) * 16] = 1.0
            out[1, part * 32 + 16 + t, t * 16 : (t + 1) * 16] = 1.0
    out[2, 101, :] = 1.0
    out[3, 103, :] = 1.0
    return out


def replicate_tables():
    cell = np.arange(128) % 32
    rep = (cell[:, None] == LANE_M[None, :]).astype(np.float32)
    sign = np.where(LANE_RI == 0, -1.0, 1.0).astype(np.float32)
    return np.stack([rep, rep * sign[None, :]])


def column_table():
    n = np.arange(256)
    ri, p, v = n // 128, (n // 32) % 4, n % 32
    angle = -2.0 * np.pi / SUB * (LANE_M[:, None] - 16.0) * (v[None, :] - 16.0)
    cos, sin = np.cos(angle), np.sin(angle)
    same = LANE_RI[:, None] == ri[None, :]
    val = np.where(same, cos, np.where(LANE_RI[:, None] == 1, -sin, sin))
    return np.where(LANE_P[:, None] == p[None, :], val, 0.0)


def row_table():
    out_ri, u = np.arange(64) // 32, np.arange(64) % 32
    in_ri, l = np.arange(64) // 32, ROW_L[np.arange(64) % 32]
    angle = -2.0 * np.pi / SUB * (u[:, None] - 16.0) * (l[None, :] - 16.0)
    cos, sin = np.cos(angle), np.sin(angle)
    same = out_ri[:, None] == in_ri[None, :]
    return np.where(same, cos, np.where(in_ri[None, :] == 1, -sin, sin))


def taper_table():
    flat = np.arange(1024)
    l, m = flat // 32, flat % 32
    one = np.sin(np.pi * (np.arange(SUB) + 0.5) / SUB)
    return (one[l] * one[m] / (K * SUB)).reshape(8, 128).astype(np.float32)


def fit_turns():
    s = (0.5 * np.cos(np.pi * (np.arange(400) + 0.5) / 800)) ** 2
    r = np.sqrt(s)
    cheb = np.polynomial.chebyshev.Chebyshev.fit
    cos = cheb(s, np.cos(2 * np.pi * r), 7, domain=[0, 0.25]).convert(kind=np.polynomial.Polynomial)
    sin = cheb(s, np.sin(2 * np.pi * r) / r, 6, domain=[0, 0.25]).convert(kind=np.polynomial.Polynomial)
    return [float(c) for c in cos.coef], [float(c) for c in sin.coef]


COS_C, SIN_C = fit_turns()


def horner(coef, s):
    acc = jnp.full_like(s, coef[-1])
    for c in coef[-2::-1]:
        acc = acc * s + c
    return acc


def cos_sin_turns(turns):
    r = turns - jnp.round(turns)
    s = r * r
    return horner(COS_C, s), horner(SIN_C, s) * r


def pack_kernel(tile_ref, vis_ref, weight_ref, meta_ref, out_ref, src_ref, count_ref):
    def clear(i, c):
        src_ref[2 * i] = -1
        src_ref[2 * i + 1] = -1
        count_ref[i] = 0
        return c

    lax.fori_loop(0, PEERS, clear, 0, unroll=8)

    def assign(s, c):
        t = tile_ref[s]
        before = count_ref[t]
        src_ref[2 * t + before] = s
        count_ref[t] = before + 1
        return c

    lax.fori_loop(0, 32, assign, 0, unroll=4)
    row = lax.broadcasted_iota(jnp.int32, (8, 256), 0)

    def one_peer(n, c):
        blocks = []
        meta = jnp.zeros((8, 256), F32)
        for j in range(2):
            s = src_ref[2 * n + j]
            valid = s >= 0
            at = jnp.maximum(s, 0)
            weighted = vis_ref[at] * weight_ref[pl.ds(at, 1), :]
            blocks.append(jnp.where(valid, weighted, 0.0))
            meta = jnp.where(jnp.logical_and(row == j, valid), meta_ref[pl.ds(at, 1), :], meta)
        blocks.append(meta)
        out_ref[n] = jnp.concatenate(blocks, axis=0).astype(BF16)
        return c

    lax.fori_loop(0, PEERS, one_peer, 0, unroll=4)


def image_kernel(recv_ref, freq_ref, spread_ref, xrow_ref, ycol_ref, i_ref, j_ref, meta_ref, du_ref, dv_ref):
    for n in range(PEERS):
        meta_ref[n] = recv_ref[n, 16:24, :].astype(F32)
    meta = meta_ref[...].reshape(256, 256).astype(BF16)
    freq = freq_ref[...]

    def spread(k):
        return jnp.dot(meta, spread_ref[k], preferred_element_type=F32)

    du_ref[...] = (spread(0) * freq + spread(2)).reshape(PEERS, 8, 256)
    dv_ref[...] = (spread(1) * freq + spread(3)).reshape(PEERS, 8, 256)
    lane = lax.broadcasted_iota(jnp.int32, (SUB, 128), 1)
    sign = jnp.where(lane < 64, -1.0, 1.0).astype(F32)

    def one_peer(n, c):
        for j in range(2):
            du = du_ref[n, j : j + 1, :]
            dv = dv_ref[n, j : j + 1, :]
            cu, su = cos_sin_turns(xrow_ref[...] * du - dv * (0.5 / SUB))
            cv, sv = cos_sin_turns(ycol_ref[...] * dv)
            left = jnp.concatenate([cu.astype(BF16), su.astype(BF16)], axis=0)
            w = recv_ref[n, 8 * j : 8 * j + 8, :].astype(F32)
            nsv = -sv
            rows = [(w[q : q + 1, :] * cv).astype(BF16) for q in range(8)]
            rows += [(w[q + 4 : q + 5, :] * nsv).astype(BF16) for q in range(4)]
            rows += [(w[q : q + 1, :] * sv).astype(BF16) for q in range(4)]
            right = jnp.concatenate(rows, axis=0)
            prod = lax.dot_general(left, right, (((1,), (1,)), ((), ())), preferred_element_type=F32)
            cc, cs = prod[:32, :128], prod[:32, 128:]
            sc, ss = prod[32:, :128], prod[32:, 128:]
            slot = 2 * n + j
            for half, (a, b) in enumerate(((cc + cs, sc + ss), (cc - cs, sc - ss))):
                image = a + sign * pltpu.roll(b, 64, 1)
                i_ref[slot, :, 128 * half : 128 * half + 128] = image
                j_ref[slot, :, 128 * half : 128 * half + 128] = pltpu.roll(image, 64, 1)
        return c

    lax.fori_loop(0, PEERS, one_peer, 0)


GROUP = 4


def grid_kernel(ints_ref, i_ref, j_ref, screen_ref, taper_ref, rep_ref, col_ref, row_ref, out_ref, acc_ref):
    acc_ref[...] = jnp.zeros(acc_ref.shape, F32)
    taper = taper_ref[...]
    lane = lax.broadcasted_iota(jnp.int32, (8, 128), 1)
    sub = lax.broadcasted_iota(jnp.int32, (8, 128), 0)
    cell = lane % 32
    group_mask = [lane // 32 == a for a in range(4)]

    def one_group(g, c):
        lhs_re, lhs_im = [], []
        for k in range(GROUP):
            base = (g * GROUP + k) * 8
            sp = screen_ref[ints_ref[base] * 32 + ints_ref[base + 1]].astype(F32)
            sq = screen_ref[ints_ref[base + 2] * 32 + ints_ref[base + 3]].astype(F32)
            pr, pi, qr, qi = sp[:8], sp[8:], sq[:8], sq[8:]
            gain_re = (pr * qr + pi * qi) * taper
            gain_im = (pr * qi - pi * qr) * taper
            lhs_re += [jnp.where(m, gain_re, 0.0) for m in group_mask]
            lhs_im += [jnp.where(m, gain_im, 0.0) for m in group_mask]
        wide_re = jnp.dot(jnp.concatenate(lhs_re, 0).astype(BF16), rep_ref[0], preferred_element_type=F32)
        wide_im = jnp.dot(jnp.concatenate(lhs_im, 0).astype(BF16), rep_ref[1], preferred_element_type=F32)
        image = i_ref[pl.ds(g * GROUP, GROUP)].reshape(GROUP * SUB, 256)
        swapped = j_ref[pl.ds(g * GROUP, GROUP)].reshape(GROUP * SUB, 256)
        corrected = (wide_re * image + wide_im * swapped).astype(BF16)
        half = jnp.dot(corrected, col_ref[...], preferred_element_type=F32).astype(BF16)
        stacked = jnp.concatenate(
            [
                jnp.concatenate([half[k * 32 : k * 32 + 32, :128], half[k * 32 : k * 32 + 32, 128:]], axis=0)
                for k in range(GROUP)
            ],
            axis=1,
        )
        cells = jnp.dot(row_ref[...], stacked, preferred_element_type=F32)
        for k in range(GROUP):
            base = (g * GROUP + k) * 8
            row8, row_shift = ints_ref[base + 4], ints_ref[base + 5]
            col32, col_shift = ints_ref[base + 6], ints_ref[base + 7]
            keep_col = cell >= col_shift
            keep_row = sub >= row_shift
            for ri in range(2):
                for part in range(4):
                    s = cells[ri * 32 + part * 8 : ri * 32 + part * 8 + 8, k * 128 : k * 128 + 128]
                    near = jnp.where(keep_col, s, 0.0)
                    far = s - near
                    for piece, at in ((near, col32), (far, col32 + 1)):
                        if part == 0:
                            top = jnp.where(keep_row, piece, 0.0)
                            acc_ref[ri, at, row8] += top
                            acc_ref[ri, at, row8 + 4] += piece - top
                        else:
                            acc_ref[ri, at, row8 + part] += piece
        return c

    lax.fori_loop(0, SLOTS // GROUP, one_group, 0)
    for band in range(16):
        for ri in range(2):
            for a in range(8):
                piece = acc_ref[ri, a, 2 * band : 2 * band + 2].reshape(16, 128)
                out_ref[band, (ri * 8 + a) * 16 : (ri * 8 + a) * 16 + 16, :] = piece.astype(BF16)


def sum_kernel(in_ref, out_ref):
    lane = lax.broadcasted_iota(jnp.int32, (16, 128), 1) // 32
    masks = [lane == a for a in range(4)]
    for ri in range(2):
        for h in range(2):
            parts = []
            for a in range(4):
                at = (ri * 8 + h * 4 + a) * 16
                total = in_ref[0, at : at + 16, :].astype(F32)
                for s in range(1, 16):
                    total = total + in_ref[s, at : at + 16, :].astype(F32)
                parts.append(total)
            for p in range(4):
                row = jnp.zeros((16, 128), F32)
                for a in range(4):
                    shift = (32 * (a - p)) % 128
                    moved = pltpu.roll(parts[a], shift, 1) if shift else parts[a]
                    row = jnp.where(masks[a], moved, row)
                out_ref[0, ri * 4 + p, :, 128 * h : 128 * h + 128] = row


VM = pl.BlockSpec(memory_space=pltpu.VMEM)
SM = pl.BlockSpec(memory_space=pltpu.SMEM)
call = functools.partial(
    pl.pallas_call, compiler_params=pltpu.CompilerParams(vmem_limit_bytes=48 << 20)
)


def pack(tile_of, visibilities, weights, meta):
    return call(
        pack_kernel,
        out_shape=jax.ShapeDtypeStruct((PEERS, 24, 256), BF16),
        in_specs=[SM, VM, VM, VM],
        out_specs=VM,
        scratch_shapes=[pltpu.SMEM((SLOTS,), jnp.int32), pltpu.SMEM((PEERS,), jnp.int32)],
        name="pack",
    )(tile_of, visibilities, weights, meta)


def images(recv, freq_row):
    xrow = np.broadcast_to(((ROW_L - 16.0) / SUB)[:, None], (SUB, 256)).astype(np.float32)
    ycol = np.broadcast_to(((np.arange(16) + 0.5) / SUB)[:, None], (16, 256)).astype(np.float32)
    shape = jax.ShapeDtypeStruct((SLOTS, SUB, 256), F32)
    return call(
        image_kernel,
        out_shape=(shape, shape),
        in_specs=[VM] * 5,
        out_specs=(VM, VM),
        scratch_shapes=[pltpu.VMEM((PEERS, 8, 256), F32)] * 3,
        name="images",
    )(recv, freq_row, jnp.asarray(spread_tables(), BF16), jnp.asarray(xrow), jnp.asarray(ycol))


def grid_tile(ints, image, swapped, screens):
    return call(
        grid_kernel,
        out_shape=jax.ShapeDtypeStruct((16, 256, 128), BF16),
        in_specs=[SM] + [VM] * 7,
        out_specs=VM,
        scratch_shapes=[pltpu.VMEM((2, 9, 33, 8, 128), F32)],
        name="grid_tile",
    )(
        ints,
        image,
        swapped,
        screens,
        jnp.asarray(taper_table()),
        jnp.asarray(replicate_tables(), BF16),
        jnp.asarray(column_table(), BF16),
        jnp.asarray(row_table(), BF16),
    )


def band_sum(arrived):
    return call(
        sum_kernel,
        out_shape=jax.ShapeDtypeStruct((1, 8, 16, 256), F32),
        in_specs=[VM],
        out_specs=VM,
        name="band_sum",
    )(arrived)


def make_meta(uv_coords, stations, offsets):
    uv = uv_coords.reshape(32, 32)
    hi = lax.reduce_precision(uv, 8, 7)
    mid = lax.reduce_precision(uv - hi, 8, 7)
    low = (uv - hi) - mid
    p, q = stations[:, 0:1], stations[:, 1:2]
    r, c = offsets[:, 0:1], offsets[:, 1:2]
    ints = [p // 32, p % 32, q // 32, q % 32, r // 8, r % 8, c // 32, c % 32]
    return jnp.concatenate(
        [hi, mid, low] + [i.astype(F32) for i in ints] + [jnp.zeros((32, 152), F32)], axis=1
    )


def on_device(visibilities, weights, uv_coords, freq_ratio, screens, stations, offsets, tile_ids):
    everyone = lax.all_gather(screens.reshape(32, 16, 128), "stat", axis=0, tiled=True)
    meta = make_meta(uv_coords, stations, offsets)
    packed = pack(tile_ids[:, 0], visibilities, weights, meta)
    recv = lax.all_to_all(packed, "tile", split_axis=0, concat_axis=0, tiled=True)
    ints = recv[:, 16:18, 96:104].astype(jnp.int32).reshape(SLOTS * 8)
    image, swapped = images(recv, jnp.tile(freq_ratio, 16)[None, :])
    partial = grid_tile(ints, image, swapped, everyone)
    arrived = lax.all_to_all(partial, "stat", split_axis=0, concat_axis=0, tiled=True)
    return band_sum(arrived)


def solution(mesh):
    placed = (
        P(("stat", "tile"), None, None),
        P(("stat", "tile"), None),
        P(("stat", "tile"), None, None),
        P(),
        P("stat", None, None),
        P(("stat", "tile"), None),
        P(("stat", "tile"), None),
        P(("stat", "tile"), None),
    )
    return jax.shard_map(
        on_device,
        mesh=mesh,
        in_specs=placed,
        out_specs=P("tile", None, "stat", None),
        check_vma=False,
    )
```

```python
import functools
import math

import jax
import jax.numpy as jnp
import numpy as np
from jax import lax
from jax.experimental import pallas as pl
from jax.experimental.pallas import tpu as pltpu
from jax.sharding import Mesh, PartitionSpec as P

SUB = 32
TS = 256
K = 256
SLOTS = 64
PEERS = 32
F32 = jnp.float32
BF16 = jnp.bfloat16

ROW_L = np.array([4 * (r % 8) + r // 8 for r in range(SUB)])
LANE = np.arange(256)
LANE_I = LANE % 16
LANE_P = (LANE // 16) % 4
LANE_RI = (LANE // 64) % 2
LANE_M = np.where(LANE < 128, 16 + LANE_I, 15 - LANE_I)


def spread_tables():
    out = np.zeros((4, 256, 256), np.float32)
    for part in range(3):
        for t in range(16):
            out[0, part * 32 + t, t * 16 : (t + 1) * 16] = 1.0
            out[1, part * 32 + 16 + t, t * 16 : (t + 1) * 16] = 1.0
    out[2, 101, :] = 1.0
    out[3, 103, :] = 1.0
    return out


def replicate_tables():
    cell = np.arange(128) % 32
    rep = (cell[:, None] == LANE_M[None, :]).astype(np.float32)
    sign = np.where(LANE_RI == 0, -1.0, 1.0).astype(np.float32)
    return np.stack([rep, rep * sign[None, :]])


def column_table():
    n = np.arange(256)
    ri, p, v = n // 128, (n // 32) % 4, n % 32
    angle = -2.0 * np.pi / SUB * (LANE_M[:, None] - 16.0) * (v[None, :] - 16.0)
    cos, sin = np.cos(angle), np.sin(angle)
    same = LANE_RI[:, None] == ri[None, :]
    val = np.where(same, cos, np.where(LANE_RI[:, None] == 1, -sin, sin))
    return np.where(LANE_P[:, None] == p[None, :], val, 0.0)


def row_table():
    out_ri, u = np.arange(64) // 32, np.arange(64) % 32
    in_ri, l = np.arange(64) // 32, ROW_L[np.arange(64) % 32]
    angle = -2.0 * np.pi / SUB * (u[:, None] - 16.0) * (l[None, :] - 16.0)
    cos, sin = np.cos(angle), np.sin(angle)
    same = out_ri[:, None] == in_ri[None, :]
    return np.where(same, cos, np.where(in_ri[None, :] == 1, -sin, sin))


def taper_table():
    flat = np.arange(1024)
    l, m = flat // 32, flat % 32
    one = np.sin(np.pi * (np.arange(SUB) + 0.5) / SUB)
    return (one[l] * one[m] / (K * SUB)).reshape(8, 128).astype(np.float32)


def fit_turns():
    s = (0.5 * np.cos(np.pi * (np.arange(400) + 0.5) / 800)) ** 2
    r = np.sqrt(s)
    cheb = np.polynomial.chebyshev.Chebyshev.fit
    cos = cheb(s, np.cos(2 * np.pi * r), 7, domain=[0, 0.25]).convert(kind=np.polynomial.Polynomial)
    sin = cheb(s, np.sin(2 * np.pi * r) / r, 6, domain=[0, 0.25]).convert(kind=np.polynomial.Polynomial)
    return [float(c) for c in cos.coef], [float(c) for c in sin.coef]


COS_C, SIN_C = fit_turns()


def horner(coef, s):
    acc = jnp.full_like(s, coef[-1])
    for c in coef[-2::-1]:
        acc = acc * s + c
    return acc


def cos_sin_turns(turns):
    r = turns - jnp.round(turns)
    s = r * r
    return horner(COS_C, s), horner(SIN_C, s) * r


def fetch(pairs, sem):
    copies = [pltpu.make_async_copy(src, dst, sem.at[i]) for i, (src, dst) in enumerate(pairs)]
    for copy in copies:
        copy.start()
    return copies


def pack_kernel(
    tile_in, vis_in, weight_in, uv_in, station_in, offset_in, out_ref,
    tile_ref, vis_ref, weight_ref, uv_ref, station_ref, offset_ref, meta_ref, src_ref, count_ref, sem,
):
    pairs = (
        (tile_in, tile_ref), (station_in, station_ref), (offset_in, offset_ref),
        (uv_in, uv_ref), (weight_in, weight_ref), (vis_in, vis_ref),
    )
    copies = fetch(pairs, sem)
    for copy in copies[:4]:
        copy.wait()
    uv = uv_ref[...]
    hi = uv.astype(BF16)
    rest = uv - hi.astype(F32)
    mid = rest.astype(BF16)
    low = (rest - mid.astype(F32)).astype(BF16)
    p, q = station_ref[0:1, :], station_ref[1:2, :]
    r, c = offset_ref[0:1, :], offset_ref[1:2, :]
    ints = jnp.concatenate([p >> 5, p & 31, q >> 5, q & 31, r >> 3, r & 7, c >> 5, c & 31], axis=0)
    columns = jnp.concatenate([hi.astype(F32), mid.astype(F32), low.astype(F32), ints.astype(F32)], axis=0)
    eye = lax.broadcasted_iota(jnp.int32, (104, 256), 0) == lax.broadcasted_iota(jnp.int32, (104, 256), 1)
    meta_ref[...] = lax.dot_general(
        columns.astype(BF16),
        eye.astype(F32).astype(BF16),
        (((0,), (0,)), ((), ())),
        preferred_element_type=F32,
    )

    def clear(i, c):
        src_ref[2 * i] = -1
        src_ref[2 * i + 1] = -1
        count_ref[i] = 0
        return c

    lax.fori_loop(0, PEERS, clear, 0, unroll=8)

    def assign(s, c):
        t = tile_ref[0, s]
        before = count_ref[t]
        src_ref[2 * t + before] = s
        count_ref[t] = before + 1
        return c

    lax.fori_loop(0, 32, assign, 0, unroll=4)
    row = lax.broadcasted_iota(jnp.int32, (8, 256), 0)
    for copy in copies[4:]:
        copy.wait()

    def one_peer(n, c):
        blocks = []
        meta = jnp.zeros((8, 256), F32)
        for j in range(2):
            s = src_ref[2 * n + j]
            valid = s >= 0
            at = jnp.maximum(s, 0)
            weighted = vis_ref[at] * weight_ref[pl.ds(at, 1), :]
            blocks.append(jnp.where(valid, weighted, 0.0))
            meta = jnp.where(jnp.logical_and(row == j, valid), meta_ref[pl.ds(at, 1), :], meta)
        blocks.append(meta)
        out_ref[n] = jnp.concatenate(blocks, axis=0).astype(BF16)
        return c

    lax.fori_loop(0, PEERS, one_peer, 0, unroll=4)


def image_kernel(
    recv_ref, freq_in, spread_in, xrow_in, ycol_in, i_ref, ints_out,
    freq_ref, spread_ref, xrow_ref, ycol_ref, ints_ref, meta_ref, du_ref, dv_ref, sem,
):
    pairs = ((freq_in, freq_ref), (spread_in, spread_ref), (xrow_in, xrow_ref), (ycol_in, ycol_ref))
    copies = fetch(pairs, sem)
    for n in range(PEERS):
        meta_ref[n] = recv_ref[n, 16:24, :].astype(F32)
    meta = meta_ref[...].reshape(256, 256).astype(BF16)
    for copy in copies:
        copy.wait()
    pick16 = lax.broadcasted_iota(jnp.int32, (16, 256), 1) % 16 == lax.broadcasted_iota(jnp.int32, (16, 256), 0)
    freq = jnp.dot(
        jnp.broadcast_to(freq_ref[...], (8, 16)),
        pick16.astype(F32),
        precision=lax.Precision.HIGHEST,
        preferred_element_type=F32,
    )[0:1]
    pick = lax.broadcasted_iota(jnp.int32, (8, 256), 0) + 96 == lax.broadcasted_iota(jnp.int32, (8, 256), 1)
    ints = lax.dot_general(
        pick.astype(F32).astype(BF16), meta, (((1,), (1,)), ((), ())), preferred_element_type=F32
    )
    ints_ref[...] = ints.astype(jnp.int32)
    send = pltpu.make_async_copy(ints_ref, ints_out, sem.at[4])
    send.start()

    def spread(k):
        return jnp.dot(meta, spread_ref[k], preferred_element_type=F32)

    du_ref[...] = (spread(0) * freq + spread(2)).reshape(PEERS, 8, 256)
    dv_ref[...] = (spread(1) * freq + spread(3)).reshape(PEERS, 8, 256)
    lane = lax.broadcasted_iota(jnp.int32, (SUB, 128), 1)
    sign = jnp.where(lane < 64, -1.0, 1.0).astype(F32)

    def one_peer(n, c):
        for j in range(2):
            du = du_ref[n, j : j + 1, :]
            dv = dv_ref[n, j : j + 1, :]
            cu, su = cos_sin_turns(xrow_ref[...] * du - dv * (0.5 / SUB))
            cv, sv = cos_sin_turns(ycol_ref[...] * dv)
            left = jnp.concatenate([cu.astype(BF16), su.astype(BF16)], axis=0)
            w = recv_ref[n, 8 * j : 8 * j + 8, :].astype(F32)
            nsv = -sv
            rows = [(w[q : q + 1, :] * cv).astype(BF16) for q in range(8)]
            rows += [(w[q + 4 : q + 5, :] * nsv).astype(BF16) for q in range(4)]
            rows += [(w[q : q + 1, :] * sv).astype(BF16) for q in range(4)]
            right = jnp.concatenate(rows, axis=0)
            prod = lax.dot_general(left, right, (((1,), (1,)), ((), ())), preferred_element_type=F32)
            cc, cs = prod[:32, :128], prod[:32, 128:]
            sc, ss = prod[32:, :128], prod[32:, 128:]
            slot = 2 * n + j
            for half, (a, b) in enumerate(((cc + cs, sc + ss), (cc - cs, sc - ss))):
                image = a + sign * pltpu.roll(b, 64, 1)
                i_ref[slot, :, 128 * half : 128 * half + 128] = image
        return c

    lax.fori_loop(0, PEERS, one_peer, 0)
    send.wait()


GROUP = 16


def grid_kernel(
    ints_in, i_ref, own_ref, other_ref, taper_in, rep_in, col_in, row_in, keep_ref, give_ref,
    ints_ref, taper_ref, rep_ref, col_ref, row_ref, acc_ref, sem,
):
    pairs = (
        (ints_in, ints_ref), (taper_in, taper_ref), (rep_in, rep_ref), (col_in, col_ref), (row_in, row_ref),
    )
    copies = fetch(pairs, sem)
    core = lax.axis_index("core")
    acc_ref[...] = jnp.zeros(acc_ref.shape, F32)
    for copy in copies:
        copy.wait()
    taper = taper_ref[...]
    lane = lax.broadcasted_iota(jnp.int32, (8, 128), 1)
    sub = lax.broadcasted_iota(jnp.int32, (8, 128), 0)
    cell = lane % 32
    group_mask = [lane // 32 == a for a in range(4)]

    def station(z_core, at):
        where = (z_core >> 1) * 32 + at
        mine = (z_core & 1) == core
        return jnp.where(mine, own_ref[where].astype(F32), other_ref[where].astype(F32))

    def one_group(g, c):
        lhs_re, lhs_im = [], []
        for k in range(GROUP):
            at = (g * (GROUP // 2) + k // 2) * 8 + k % 2
            sp = station(ints_ref[0, at], ints_ref[1, at])
            sq = station(ints_ref[2, at], ints_ref[3, at])
            pr, pi, qr, qi = sp[:8], sp[8:], sq[:8], sq[8:]
            gain_re = (pr * qr + pi * qi) * taper
            gain_im = (pr * qi - pi * qr) * taper
            lhs_re += [jnp.where(m, gain_re, 0.0) for m in group_mask]
            lhs_im += [jnp.where(m, gain_im, 0.0) for m in group_mask]
        wide_re = jnp.dot(jnp.concatenate(lhs_re, 0).astype(BF16), rep_ref[0], preferred_element_type=F32)
        wide_im = jnp.dot(jnp.concatenate(lhs_im, 0).astype(BF16), rep_ref[1], preferred_element_type=F32)
        image = i_ref[pl.ds(g * GROUP, GROUP)].reshape(GROUP * SUB, 256)
        swapped = jnp.concatenate([pltpu.roll(image[:, :128], 64, 1), pltpu.roll(image[:, 128:], 64, 1)], axis=1)
        corrected = (wide_re * image + wide_im * swapped).astype(BF16)
        half = jnp.dot(corrected, col_ref[...], preferred_element_type=F32).astype(BF16)
        stacked = jnp.concatenate(
            [
                jnp.concatenate([half[k * 32 : k * 32 + 32, :128], half[k * 32 : k * 32 + 32, 128:]], axis=0)
                for k in range(GROUP)
            ],
            axis=1,
        )
        cells = jnp.dot(row_ref[...], stacked, preferred_element_type=F32)
        for k in range(GROUP):
            at = (g * (GROUP // 2) + k // 2) * 8 + k % 2
            row8, row_shift = ints_ref[4, at], ints_ref[5, at]
            col32, col_shift = ints_ref[6, at], ints_ref[7, at]
            keep_col = cell >= col_shift
            keep_row = sub >= row_shift
            for ri in range(2):
                for part in range(4):
                    s = cells[ri * 32 + part * 8 : ri * 32 + part * 8 + 8, k * 128 : k * 128 + 128]
                    near = jnp.where(keep_col, s, 0.0)
                    far = s - near
                    for piece, block in ((near, col32), (far, col32 + 1)):
                        if part == 0:
                            top = jnp.where(keep_row, piece, 0.0)
                            acc_ref[ri, block, row8] += top
                            acc_ref[ri, block, row8 + 4] += piece - top
                        else:
                            acc_ref[ri, block, row8 + part] += piece
        return c

    lax.fori_loop(0, SLOTS // GROUP, one_group, 0)
    for z in range(8):
        for ri in range(2):
            for a in range(8):
                at = (ri * 8 + a) * 16
                keep = acc_ref[ri, a, pl.ds(4 * z + 2 * core, 2)].reshape(16, 128)
                give = acc_ref[ri, a, pl.ds(4 * z + 2 - 2 * core, 2)].reshape(16, 128)
                keep_ref[z, at : at + 16, :] = keep.astype(BF16)
                give_ref[z, at : at + 16, :] = give.astype(BF16)


def sum_kernel(in_ref, out_ref):
    lane = lax.broadcasted_iota(jnp.int32, (16, 128), 1) // 32
    masks = [lane == a for a in range(4)]
    for ri in range(2):
        for h in range(2):
            parts = []
            for a in range(4):
                at = (ri * 8 + h * 4 + a) * 16
                total = in_ref[0, at : at + 16, :].astype(F32)
                for s in range(1, 8):
                    total = total + in_ref[s, at : at + 16, :].astype(F32)
                parts.append(total)
            for p in range(4):
                row = jnp.zeros((16, 128), F32)
                for a in range(4):
                    shift = (32 * (a - p)) % 128
                    moved = pltpu.roll(parts[a], shift, 1) if shift else parts[a]
                    row = jnp.where(masks[a], moved, row)
                out_ref[0, ri * 4 + p, :, 128 * h : 128 * h + 128] = row


VM = pl.BlockSpec(memory_space=pltpu.VMEM)
SM = pl.BlockSpec(memory_space=pltpu.SMEM)
HBM = pl.BlockSpec(memory_space=pltpu.HBM)
call = functools.partial(
    pl.pallas_call, compiler_params=pltpu.CompilerParams(vmem_limit_bytes=16 << 20)
)


def pinned(x):
    return pltpu.with_memory_space_constraint(x, pltpu.HBM)


def pack(tile_of, visibilities, weights, uv, stations, offsets):
    args = (tile_of, visibilities, weights, uv, stations, offsets)
    args = tuple(pinned(a) for a in args)
    return call(
        pack_kernel,
        out_shape=jax.ShapeDtypeStruct((PEERS, 24, 256), BF16),
        in_specs=[HBM] * 6,
        out_specs=VM,
        scratch_shapes=[pltpu.SMEM(tile_of.shape, jnp.int32)]
        + [pltpu.VMEM(a.shape, a.dtype) for a in args[1:]]
        + [
            pltpu.VMEM((32, 256), F32),
            pltpu.SMEM((SLOTS,), jnp.int32),
            pltpu.SMEM((PEERS,), jnp.int32),
            pltpu.SemaphoreType.DMA((6,)),
        ],
        name="pack",
    )(*args)


def images(recv, freq):
    xrow = np.broadcast_to(((ROW_L - 16.0) / SUB)[:, None], (SUB, 256)).astype(np.float32)
    ycol = np.broadcast_to(((np.arange(16) + 0.5) / SUB)[:, None], (16, 256)).astype(np.float32)
    args = (freq, jnp.asarray(spread_tables(), BF16), jnp.asarray(xrow), jnp.asarray(ycol))
    return call(
        image_kernel,
        out_shape=(
            jax.ShapeDtypeStruct((SLOTS, SUB, 256), F32),
            jax.ShapeDtypeStruct((8, 256), jnp.int32),
        ),
        in_specs=[VM] + [HBM] * 4,
        out_specs=(VM, HBM),
        scratch_shapes=[pltpu.VMEM(a.shape, a.dtype) for a in args]
        + [pltpu.VMEM((8, 256), jnp.int32)]
        + [pltpu.VMEM((PEERS, 8, 256), F32)] * 3
        + [pltpu.SemaphoreType.DMA((5,))],
        name="images",
    )(recv, *[pinned(a) for a in args])


def grid_tile(ints, image, own, other):
    shape = jax.ShapeDtypeStruct((8, 256, 128), BF16)
    tables = (
        jnp.asarray(taper_table()),
        jnp.asarray(replicate_tables(), BF16),
        jnp.asarray(column_table(), BF16),
        jnp.asarray(row_table(), BF16),
    )
    return call(
        grid_kernel,
        out_shape=(shape, shape),
        in_specs=[HBM, VM, VM, VM] + [HBM] * 4,
        out_specs=(VM, VM),
        scratch_shapes=[pltpu.SMEM(ints.shape, jnp.int32)]
        + [pltpu.VMEM(t.shape, t.dtype) for t in tables]
        + [pltpu.VMEM((2, 9, 33, 8, 128), F32), pltpu.SemaphoreType.DMA((5,))],
        name="grid_tile",
    )(pinned(ints), image, own, other, *[pinned(t) for t in tables])


def band_sum(arrived):
    return call(
        sum_kernel,
        out_shape=jax.ShapeDtypeStruct((1, 8, 16, 256), F32),
        in_specs=[VM],
        out_specs=VM,
        name="band_sum",
    )(arrived)


SWAP = [(0, 1), (1, 0)]


def on_device(visibilities, weights, uv_coords, freq_ratio, screens, stations, offsets, tile_ids):
    uv = jnp.transpose(uv_coords, (1, 2, 0)).reshape(32, 32)
    packed = pack(tile_ids.T, visibilities, weights, uv, stations.T, offsets.T)
    recv = lax.all_to_all(packed, "tile", split_axis=0, concat_axis=0, tiled=True)
    mine = jnp.broadcast_to(screens.reshape(1, 32, 16, 128), (8, 32, 16, 128))
    own = lax.all_to_all(mine, "z", split_axis=0, concat_axis=0, tiled=True).reshape(256, 16, 128)
    image, ints = images(recv, freq_ratio[None, :])
    own, image = lax.optimization_barrier((own, image))
    other = lax.ppermute(own, "core", SWAP)
    keep, give = grid_tile(ints, image, own, other)
    taken = lax.ppermute(give, "core", SWAP)
    both = (keep.astype(F32) + taken.astype(F32)).astype(BF16)
    arrived = lax.all_to_all(both, "z", split_axis=0, concat_axis=0, tiled=True)
    return band_sum(arrived)


def solution(mesh):
    stat, tile = mesh.shape["stat"], mesh.shape["tile"]
    fine = Mesh(mesh.devices.reshape(stat // 2, 2, tile), ("z", "core", "tile"))
    every = ("z", "core", "tile")
    placed = (
        P(every, None, None),
        P(every, None),
        P(every, None, None),
        P(),
        P(("z", "core"), None, None),
        P(every, None),
        P(every, None),
        P(every, None),
    )
    return jax.shard_map(
        on_device,
        mesh=fine,
        in_specs=placed,
        out_specs=P("tile", None, ("z", "core"), None),
        check_vma=False,
    )
```

```python
import functools
import math

import jax
import jax.numpy as jnp
import numpy as np
from jax import lax
from jax.experimental import pallas as pl
from jax.experimental.pallas import tpu as pltpu
from jax.sharding import Mesh, PartitionSpec as P

SUB = 32
TS = 256
K = 256
SLOTS = 64
PEERS = 32
F32 = jnp.float32
BF16 = jnp.bfloat16

ROW_L = np.array([4 * (r % 8) + r // 8 for r in range(SUB)])
LANE = np.arange(128)
LANE_I = LANE % 16
LANE_P = (LANE // 16) % 2
LANE_RI = LANE // 64
LANE_M = np.where((LANE // 32) % 2 == 0, 16 + LANE_I, 15 - LANE_I)


def spread_tables():
    out = np.zeros((4, 256, 256), np.float32)
    for part in range(3):
        for t in range(16):
            out[0, part * 32 + t, t * 16 : (t + 1) * 16] = 1.0
            out[1, part * 32 + 16 + t, t * 16 : (t + 1) * 16] = 1.0
    out[2, 101, :] = 1.0
    out[3, 103, :] = 1.0
    return out


def replicate_tables():
    cell = np.arange(128) % 32
    rep = (cell[:, None] == LANE_M[None, :]).astype(np.float32)
    sign = np.where(LANE_RI == 0, -1.0, 1.0).astype(np.float32)
    return np.stack([rep, rep * sign[None, :]])


def column_table():
    n = np.arange(256)
    twice, ri, p, v = n // 128, (n // 64) % 2, (n // 32) % 2, n % 32
    turns = -(LANE_M[:, None] - 16.0) * (v[None, :] - 16.0) / SUB
    turns = turns + 0.25 * (twice[None, :] - ri[None, :] + LANE_RI[:, None])
    val = np.cos(2.0 * np.pi * turns)
    return np.where(LANE_P[:, None] == p[None, :], val, 0.0)


def row_table():
    u, part, l = np.arange(32), np.arange(64) // 32, ROW_L[np.arange(64) % 32]
    angle = -2.0 * np.pi / SUB * (u[:, None] - 16.0) * (l[None, :] - 16.0)
    return np.where(part[None, :] == 0, np.cos(angle), np.sin(angle))


def taper_table():
    flat = np.arange(1024)
    l, m = flat // 32, flat % 32
    one = np.sin(np.pi * (np.arange(SUB) + 0.5) / SUB)
    return (one[l] * one[m] / (K * SUB)).reshape(8, 128).astype(np.float32)


def fit_turns():
    s = (0.5 * np.cos(np.pi * (np.arange(400) + 0.5) / 800)) ** 2
    r = np.sqrt(s)
    cheb = np.polynomial.chebyshev.Chebyshev.fit
    cos = cheb(s, np.cos(2 * np.pi * r), 6, domain=[0, 0.25]).convert(kind=np.polynomial.Polynomial)
    sin = cheb(s, np.sin(2 * np.pi * r) / r, 5, domain=[0, 0.25]).convert(kind=np.polynomial.Polynomial)
    return [float(c) for c in cos.coef], [float(c) for c in sin.coef]


COS_C, SIN_C = fit_turns()


def horner(coef, s):
    acc = jnp.full_like(s, coef[-1])
    for c in coef[-2::-1]:
        acc = acc * s + c
    return acc


def cos_sin_turns(turns):
    r = turns - jnp.round(turns)
    s = r * r
    return horner(COS_C, s), horner(SIN_C, s) * r


def fetch(pairs, sem):
    copies = [pltpu.make_async_copy(src, dst, sem.at[i]) for i, (src, dst) in enumerate(pairs)]
    for copy in copies:
        copy.start()
    return copies


def pack_kernel(
    tile_in, vis_in, weight_in, uv_in, station_in, offset_in, screen_in, out_ref, mine_out,
    tile_ref, vis_ref, weight_ref, uv_ref, station_ref, offset_ref, screen_ref,
    meta_ref, wide_ref, mine_ref, src_ref, count_ref, sem,
):
    pairs = (
        (tile_in, tile_ref), (station_in, station_ref), (offset_in, offset_ref),
        (uv_in, uv_ref), (weight_in, weight_ref), (vis_in, vis_ref), (screen_in, screen_ref),
    )
    copies = fetch(pairs, sem)
    for copy in copies[:4]:
        copy.wait()
    uv = uv_ref[...]
    hi = uv.astype(BF16)
    rest = uv - hi.astype(F32)
    mid = rest.astype(BF16)
    low = (rest - mid.astype(F32)).astype(BF16)
    p, q = station_ref[0:1, :], station_ref[1:2, :]
    r, c = offset_ref[0:1, :], offset_ref[1:2, :]
    ints = jnp.concatenate([p >> 5, p & 31, q >> 5, q & 31, r >> 3, r & 7, c >> 5, c & 31], axis=0)
    columns = jnp.concatenate([hi.astype(F32), mid.astype(F32), low.astype(F32), ints.astype(F32)], axis=0)
    eye = lax.broadcasted_iota(jnp.int32, (104, 256), 0) == lax.broadcasted_iota(jnp.int32, (104, 256), 1)
    meta_ref[...] = lax.dot_general(
        columns.astype(BF16),
        eye.astype(F32).astype(BF16),
        (((0,), (0,)), ((), ())),
        preferred_element_type=F32,
    )

    def clear(i, c):
        src_ref[2 * i] = -1
        src_ref[2 * i + 1] = -1
        count_ref[i] = 0
        return c

    lax.fori_loop(0, PEERS, clear, 0, unroll=8)

    def assign(s, c):
        t = tile_ref[0, s]
        before = count_ref[t]
        src_ref[2 * t + before] = s
        count_ref[t] = before + 1
        return c

    lax.fori_loop(0, 32, assign, 0, unroll=4)
    row = lax.broadcasted_iota(jnp.int32, (8, 256), 0)
    for copy in copies[4:6]:
        copy.wait()

    def one_peer(n, c):
        low, high = [], []
        meta = jnp.zeros((8, 256), F32)
        for j in range(2):
            s = src_ref[2 * n + j]
            valid = s >= 0
            at = jnp.maximum(s, 0)
            weighted = jnp.where(valid, vis_ref[at] * weight_ref[pl.ds(at, 1), :], 0.0)
            low += [weighted[0:2], weighted[4:6]]
            high += [weighted[2:4], weighted[6:8]]
            meta = jnp.where(jnp.logical_and(row == j, valid), meta_ref[pl.ds(at, 1), :], meta)
        out_ref[n] = jnp.concatenate(low + high + [meta], axis=0).astype(BF16)
        return c

    lax.fori_loop(0, PEERS, one_peer, 0, unroll=4)
    copies[6].wait()
    wide_ref[...] = screen_ref[...].astype(F32).reshape(512, 128)
    parts = [wide_ref[pl.ds(ri, 256, stride=2), :].reshape(32, 8, 128) for ri in range(2)]
    mine_ref[...] = jnp.concatenate(parts, axis=1).astype(BF16)
    sends = fetch([(mine_ref, mine_out.at[z]) for z in range(8)], sem)
    for send in sends:
        send.wait()


def image_kernel(
    recv_ref, other_ref, freq_in, spread_in, xrow_in, ycol_in, i_ref, ints_out,
    freq_ref, spread_ref, xrow_ref, ycol_ref, ints_ref, meta_ref, du_ref, dv_ref, sem,
):
    pairs = ((freq_in, freq_ref), (spread_in, spread_ref), (xrow_in, xrow_ref), (ycol_in, ycol_ref))
    copies = fetch(pairs, sem)
    core = lax.axis_index("core")
    for b, block_ref in enumerate((recv_ref, other_ref)):
        for n in range(PEERS):
            meta_ref[b * PEERS + n] = block_ref[3 * n + 2].astype(F32)
    meta = meta_ref[...].reshape(512, 256).astype(BF16)
    for copy in copies:
        copy.wait()
    pick16 = lax.broadcasted_iota(jnp.int32, (16, 256), 1) % 16 == lax.broadcasted_iota(jnp.int32, (16, 256), 0)
    freq = jnp.dot(
        jnp.broadcast_to(freq_ref[...], (8, 16)),
        pick16.astype(F32),
        precision=lax.Precision.HIGHEST,
        preferred_element_type=F32,
    )[0:1]
    pick = lax.broadcasted_iota(jnp.int32, (8, 256), 0) + 96 == lax.broadcasted_iota(jnp.int32, (8, 256), 1)
    ints = lax.dot_general(
        pick.astype(F32).astype(BF16), meta, (((1,), (1,)), ((), ())), preferred_element_type=F32
    )
    ints_ref[...] = ints.astype(jnp.int32)
    send = pltpu.make_async_copy(ints_ref, ints_out, sem.at[4])
    send.start()

    def spread(k):
        return jnp.dot(meta, spread_ref[k], preferred_element_type=F32)

    du_ref[...] = (spread(0) * freq + spread(2)).reshape(2 * PEERS, 8, 256)
    dv_ref[...] = (spread(1) * freq + spread(3)).reshape(2 * PEERS, 8, 256)

    def one_slot(block_ref, row, n, j, slot):
        du = du_ref[row, j : j + 1, :]
        dv = dv_ref[row, j : j + 1, :]
        cu, su = cos_sin_turns(xrow_ref[...] * du - dv * (0.5 / SUB))
        cv, sv = cos_sin_turns(ycol_ref[...] * dv)
        left = jnp.concatenate([cu.astype(BF16), su.astype(BF16)], axis=1)
        w = block_ref[3 * n + core].astype(F32)[4 * j : 4 * j + 4, :]
        table = {}
        for p in range(2):
            re, im = w[p : p + 1, :], w[2 + p : 3 + p, :]
            for ri, (a, b) in enumerate(((re * cv, im * sv), (im * cv, re * sv))):
                minus, plus = (a - b).astype(BF16), (a + b).astype(BF16)
                table[ri, 0, p] = minus if ri == 0 else plus
                table[ri, 1, p] = plus if ri == 0 else minus
        keys = [(ri, s, p) for ri in range(2) for s in range(2) for p in range(2)]
        direct = jnp.concatenate([table[key] for key in keys], axis=0)
        turned = jnp.concatenate([-table[1, s, p] if ri == 0 else table[0, s, p] for ri, s, p in keys], axis=0)
        right = jnp.concatenate([direct, turned], axis=1)
        i_ref[slot] = lax.dot_general(left, right, (((1,), (1,)), ((), ())), preferred_element_type=F32)

    def one_peer(n, c):
        for b, block_ref in enumerate((recv_ref, other_ref)):
            for j in range(2):
                one_slot(block_ref, b * PEERS + n, n, j, 4 * n + 2 * b + j)
        return c

    lax.fori_loop(0, PEERS, one_peer, 0, unroll=2)
    send.wait()


GROUP = 32


def grid_kernel(
    ints_in, i_ref, own_ref, other_ref, taper_in, rep_in, col_in, row_in, out_ref,
    ints_ref, taper_ref, rep_ref, col_ref, row_ref, acc_ref, sem,
):
    pairs = (
        (ints_in, ints_ref), (taper_in, taper_ref), (rep_in, rep_ref), (col_in, col_ref), (row_in, row_ref),
    )
    copies = fetch(pairs, sem)
    core = lax.axis_index("core")
    acc_ref[...] = jnp.zeros(acc_ref.shape, F32)
    for copy in copies:
        copy.wait()
    taper = taper_ref[...]
    lane = lax.broadcasted_iota(jnp.int32, (8, 128), 1)
    sub = lax.broadcasted_iota(jnp.int32, (8, 128), 0)
    cell = lane % 32
    lane16 = lax.broadcasted_iota(jnp.int32, (16, 128), 1) // 32
    upper = lax.broadcasted_iota(jnp.int32, (16, 128), 0) // 8
    group_mask = [(lane16 == 2 * a + upper).astype(F32).astype(BF16) for a in range(2)]

    def station(z_core, at):
        where = (z_core >> 1) * 32 + at
        mine = (z_core & 1) == core
        return jnp.where(mine, own_ref[where], other_ref[where]).astype(F32)

    def place(g, k):
        return (k // 2 % 2) * 256 + (g * (GROUP // 4) + k // 4) * 8 + k % 2

    def one_group(g, c):
        lhs_re, lhs_im = [], []
        for k in range(GROUP):
            at = place(g, k)
            sp = station(ints_ref[0, at], ints_ref[1, at])
            sq = station(ints_ref[2, at], ints_ref[3, at])
            pr, pi, qr, qi = sp[:8], sp[8:], sq[:8], sq[8:]
            gain_re = (pr * qr + pi * qi) * taper
            gain_im = (pr * qi - pi * qr) * taper
            twice_re = jnp.concatenate([gain_re, gain_re], 0).astype(BF16)
            twice_im = jnp.concatenate([gain_im, gain_im], 0).astype(BF16)
            lhs_re += [twice_re * m for m in group_mask]
            lhs_im += [twice_im * m for m in group_mask]
        wide_re = jnp.dot(jnp.concatenate(lhs_re, 0), rep_ref[0], preferred_element_type=F32)
        wide_im = jnp.dot(jnp.concatenate(lhs_im, 0), rep_ref[1], preferred_element_type=F32)
        image = i_ref[pl.ds(g * GROUP, GROUP)].reshape(GROUP * SUB, 128)
        swapped = pltpu.roll(image, 64, 1)
        corrected = (wide_re * image + wide_im * swapped).astype(BF16)
        half = jnp.dot(corrected, col_ref[...], preferred_element_type=F32).astype(BF16)
        stacked = jnp.concatenate(
            [
                jnp.concatenate([half[k * 32 : k * 32 + 32, :128], half[k * 32 : k * 32 + 32, 128:]], axis=0)
                for k in range(GROUP)
            ],
            axis=1,
        )
        cells = jnp.dot(row_ref[...], stacked, preferred_element_type=F32)
        for k in range(GROUP):
            at = place(g, k)
            row8, row_shift = ints_ref[4, at], ints_ref[5, at]
            col32, col_shift = ints_ref[6, at], ints_ref[7, at]
            keep_col = cell >= col_shift
            keep_row = sub >= row_shift
            for part in range(4):
                s = cells[part * 8 : part * 8 + 8, k * 128 : k * 128 + 128]
                near = jnp.where(keep_col, s, 0.0)
                far = s - near
                for piece, block in ((near, col32), (far, col32 + 1)):
                    if part == 0:
                        top = jnp.where(keep_row, piece, 0.0)
                        acc_ref[block, row8] += top
                        acc_ref[block, row8 + 4] += piece - top
                    else:
                        acc_ref[block, row8 + part] += piece
        return c

    lax.fori_loop(0, 2 * SLOTS // GROUP, one_group, 0)
    for band in range(16):
        for a in range(8):
            piece = acc_ref[a, 2 * band : 2 * band + 2].reshape(16, 128)
            out_ref[band, a * 16 : a * 16 + 16, :] = piece.astype(BF16)


def sum_kernel(in_ref, out_ref):
    lane = lax.broadcasted_iota(jnp.int32, (16, 128), 1) // 32
    masks = [lane == a for a in range(4)]
    for core in range(2):
        for h in range(2):
            parts = []
            for a in range(4):
                at = (h * 4 + a) * 16
                total = in_ref[core, at : at + 16, :].astype(F32)
                for z in range(1, 8):
                    total = total + in_ref[2 * z + core, at : at + 16, :].astype(F32)
                parts.append(total)
            for g in range(4):
                row = jnp.zeros((16, 128), F32)
                for a in range(4):
                    shift = (32 * (a - g)) % 128
                    moved = pltpu.roll(parts[a], shift, 1) if shift else parts[a]
                    row = jnp.where(masks[a], moved, row)
                out_ref[0, (g // 2) * 4 + 2 * core + g % 2, :, 128 * h : 128 * h + 128] = row


VM = pl.BlockSpec(memory_space=pltpu.VMEM)
SM = pl.BlockSpec(memory_space=pltpu.SMEM)
HBM = pl.BlockSpec(memory_space=pltpu.HBM)
call = functools.partial(
    pl.pallas_call, compiler_params=pltpu.CompilerParams(vmem_limit_bytes=16 << 20)
)


def pinned(x):
    return pltpu.with_memory_space_constraint(x, pltpu.HBM)


def pack(*args):
    return call(
        pack_kernel,
        out_shape=(
            jax.ShapeDtypeStruct((PEERS, 24, 256), BF16),
            jax.ShapeDtypeStruct((8, 32, 16, 128), BF16),
        ),
        in_specs=[HBM] * 7,
        out_specs=(VM, HBM),
        scratch_shapes=[pltpu.SMEM(args[0].shape, jnp.int32)]
        + [pltpu.VMEM(a.shape, a.dtype) for a in args[1:]]
        + [
            pltpu.VMEM((32, 256), F32),
            pltpu.VMEM((512, 128), F32),
            pltpu.VMEM((32, 16, 128), BF16),
            pltpu.SMEM((SLOTS,), jnp.int32),
            pltpu.SMEM((PEERS,), jnp.int32),
            pltpu.SemaphoreType.DMA((8,)),
        ],
        name="pack",
    )(*[pinned(a) for a in args])


def images(recv, sibling, freq):
    xrow = np.broadcast_to(((ROW_L - 16.0) / SUB)[:, None], (SUB, 256)).astype(np.float32)
    ycol = np.broadcast_to(((np.arange(16) + 0.5) / SUB)[:, None], (16, 256)).astype(np.float32)
    args = (freq, jnp.asarray(spread_tables(), BF16), jnp.asarray(xrow), jnp.asarray(ycol))
    return call(
        image_kernel,
        out_shape=(
            jax.ShapeDtypeStruct((2 * SLOTS, SUB, 128), F32),
            jax.ShapeDtypeStruct((8, 512), jnp.int32),
        ),
        in_specs=[VM, VM] + [HBM] * 4,
        out_specs=(VM, HBM),
        scratch_shapes=[pltpu.VMEM(a.shape, a.dtype) for a in args]
        + [pltpu.VMEM((8, 512), jnp.int32)]
        + [pltpu.VMEM((2 * PEERS, 8, 256), F32)] * 3
        + [pltpu.SemaphoreType.DMA((5,))],
        name="images",
    )(recv, sibling, *[pinned(a) for a in args])


def grid_tile(ints, image, own, other):
    tables = (
        jnp.asarray(taper_table()),
        jnp.asarray(replicate_tables(), BF16),
        jnp.asarray(column_table(), BF16),
        jnp.asarray(row_table(), BF16),
    )
    return call(
        grid_kernel,
        out_shape=jax.ShapeDtypeStruct((16, 128, 128), BF16),
        in_specs=[HBM, VM, VM, VM] + [HBM] * 4,
        out_specs=VM,
        scratch_shapes=[pltpu.SMEM(ints.shape, jnp.int32)]
        + [pltpu.VMEM(t.shape, t.dtype) for t in tables]
        + [pltpu.VMEM((9, 33, 8, 128), F32), pltpu.SemaphoreType.DMA((5,))],
        name="grid_tile",
    )(pinned(ints), image, own, other, *[pinned(t) for t in tables])


def band_sum(arrived):
    return call(
        sum_kernel,
        out_shape=jax.ShapeDtypeStruct((1, 8, 16, 256), F32),
        in_specs=[VM],
        out_specs=VM,
        name="band_sum",
    )(arrived)


SWAP = [(0, 1), (1, 0)]


def on_device(visibilities, weights, uv_coords, freq_ratio, screens, stations, offsets, tile_ids):
    uv = jnp.transpose(uv_coords, (1, 2, 0)).reshape(32, 32)
    pairs = jnp.transpose(screens.reshape(32, 2, 8, 128), (0, 2, 1, 3)).reshape(32, 16, 128)
    packed, mine = pack(tile_ids.T, visibilities, weights, uv, stations.T, offsets.T, pairs)
    recv = lax.all_to_all(packed, "tile", split_axis=0, concat_axis=0, tiled=True)
    own = lax.all_to_all(mine, "z", split_axis=0, concat_axis=0, tiled=True).reshape(256, 16, 128)
    sibling = lax.ppermute(recv, "core", SWAP)
    image, ints = images(recv.reshape(96, 8, 256), sibling.reshape(96, 8, 256), freq_ratio[None, :])
    own, image = lax.optimization_barrier((own, image))
    other = lax.ppermute(own, "core", SWAP)
    partial = grid_tile(ints, image, own, other)
    arrived = lax.all_to_all(partial, ("z", "core"), split_axis=0, concat_axis=0, tiled=True)
    return band_sum(arrived)


def solution(mesh):
    stat, tile = mesh.shape["stat"], mesh.shape["tile"]
    fine = Mesh(mesh.devices.reshape(stat // 2, 2, tile), ("z", "core", "tile"))
    every = ("z", "core", "tile")
    placed = (
        P(every, None, None),
        P(every, None),
        P(every, None, None),
        P(),
        P(("z", "core"), None, None),
        P(every, None),
        P(every, None),
        P(every, None),
    )
    return jax.shard_map(
        on_device,
        mesh=fine,
        in_specs=placed,
        out_specs=P("tile", None, ("z", "core"), None),
        check_vma=False,
    )
```

```python
import functools
import math

import jax
import jax.numpy as jnp
import numpy as np
from jax import lax
from jax.experimental import pallas as pl
from jax.experimental.pallas import tpu as pltpu
from jax.sharding import Mesh, PartitionSpec as P

SUB = 32
TS = 256
K = 256
SLOTS = 64
PEERS = 32
F32 = jnp.float32
BF16 = jnp.bfloat16

ROW_L = np.array([4 * (r % 8) + r // 8 for r in range(SUB)])
LANE = np.arange(128)
LANE_I = LANE % 16
LANE_P = (LANE // 16) % 2
LANE_RI = LANE // 64
LANE_M = np.where((LANE // 32) % 2 == 0, 16 + LANE_I, 15 - LANE_I)


def spread_tables():
    out = np.zeros((4, 256, 256), np.float32)
    for part in range(3):
        for t in range(16):
            out[0, part * 32 + t, t * 16 : (t + 1) * 16] = 1.0
            out[1, part * 32 + 16 + t, t * 16 : (t + 1) * 16] = 1.0
    out[2, 101, :] = 1.0
    out[3, 103, :] = 1.0
    return out


def replicate_tables():
    cell = np.arange(128) % 32
    rep = (cell[:, None] == LANE_M[None, :]).astype(np.float32)
    sign = np.where(LANE_RI == 0, -1.0, 1.0).astype(np.float32)
    return np.stack([rep, rep * sign[None, :]])


def column_table():
    n = np.arange(256)
    twice, ri, p, v = n // 128, (n // 64) % 2, (n // 32) % 2, n % 32
    turns = -(LANE_M[:, None] - 16.0) * (v[None, :] - 16.0) / SUB
    turns = turns + 0.25 * (twice[None, :] - ri[None, :] + LANE_RI[:, None])
    val = np.cos(2.0 * np.pi * turns)
    return np.where(LANE_P[:, None] == p[None, :], val, 0.0)


def row_table():
    u, part, l = np.arange(32), np.arange(64) // 32, ROW_L[np.arange(64) % 32]
    angle = -2.0 * np.pi / SUB * (u[:, None] - 16.0) * (l[None, :] - 16.0)
    return np.where(part[None, :] == 0, np.cos(angle), np.sin(angle))


def taper_table():
    flat = np.arange(1024)
    l, m = flat // 32, flat % 32
    one = np.sin(np.pi * (np.arange(SUB) + 0.5) / SUB)
    return (one[l] * one[m] / (K * SUB)).reshape(8, 128).astype(np.float32)


def fit_turns():
    s = (0.5 * np.cos(np.pi * (np.arange(400) + 0.5) / 800)) ** 2
    r = np.sqrt(s)
    cheb = np.polynomial.chebyshev.Chebyshev.fit
    cos = cheb(s, np.cos(2 * np.pi * r), 6, domain=[0, 0.25]).convert(kind=np.polynomial.Polynomial)
    sin = cheb(s, np.sin(2 * np.pi * r) / r, 5, domain=[0, 0.25]).convert(kind=np.polynomial.Polynomial)
    return [float(c) for c in cos.coef], [float(c) for c in sin.coef]


COS_C, SIN_C = fit_turns()


def horner(coef, s):
    acc = jnp.full_like(s, coef[-1])
    for c in coef[-2::-1]:
        acc = acc * s + c
    return acc


def cos_sin_turns(turns):
    r = turns - jnp.round(turns)
    s = r * r
    return horner(COS_C, s), horner(SIN_C, s) * r


def fetch(pairs, sem):
    copies = [pltpu.make_async_copy(src, dst, sem.at[i]) for i, (src, dst) in enumerate(pairs)]
    for copy in copies:
        copy.start()
    return copies


def pack_kernel(
    tile_in, vis_in, weight_in, uv_in, station_in, offset_in, screen_in, out_ref, mine_ref,
    tile_ref, vis_ref, weight_ref, uv_ref, station_ref, offset_ref, screen_ref,
    meta_ref, wide_ref, src_ref, count_ref, sem,
):
    pairs = (
        (tile_in, tile_ref), (station_in, station_ref), (offset_in, offset_ref),
        (uv_in, uv_ref), (weight_in, weight_ref), (vis_in, vis_ref), (screen_in.at[pl.ds(8 * lax.axis_index("x"), 8)], screen_ref),
    )
    copies = fetch(pairs, sem)
    for copy in copies[:4]:
        copy.wait()
    uv = uv_ref[...]
    hi = uv.astype(BF16)
    rest = uv - hi.astype(F32)
    mid = rest.astype(BF16)
    low = (rest - mid.astype(F32)).astype(BF16)
    p, q = station_ref[0:1, :], station_ref[1:2, :]
    r, c = offset_ref[0:1, :], offset_ref[1:2, :]
    ints = jnp.concatenate([p >> 5, p & 31, q >> 5, q & 31, r >> 3, r & 7, c >> 5, c & 31], axis=0)
    columns = jnp.concatenate([hi.astype(F32), mid.astype(F32), low.astype(F32), ints.astype(F32)], axis=0)
    eye = lax.broadcasted_iota(jnp.int32, (104, 256), 0) == lax.broadcasted_iota(jnp.int32, (104, 256), 1)
    meta_ref[...] = lax.dot_general(
        columns.astype(BF16),
        eye.astype(F32).astype(BF16),
        (((0,), (0,)), ((), ())),
        preferred_element_type=F32,
    )

    def clear(i, c):
        src_ref[2 * i] = -1
        src_ref[2 * i + 1] = -1
        count_ref[i] = 0
        return c

    lax.fori_loop(0, PEERS, clear, 0, unroll=8)

    def assign(s, c):
        t = tile_ref[0, s]
        before = count_ref[t]
        src_ref[2 * t + before] = s
        count_ref[t] = before + 1
        return c

    lax.fori_loop(0, 32, assign, 0, unroll=4)
    row = lax.broadcasted_iota(jnp.int32, (8, 256), 0)
    for copy in copies[4:6]:
        copy.wait()

    def one_peer(n, c):
        low, high = [], []
        meta = jnp.zeros((8, 256), F32)
        for j in range(2):
            s = src_ref[2 * n + j]
            valid = s >= 0
            at = jnp.maximum(s, 0)
            weighted = jnp.where(valid, vis_ref[at] * weight_ref[pl.ds(at, 1), :], 0.0)
            low += [weighted[0:2], weighted[4:6]]
            high += [weighted[2:4], weighted[6:8]]
            meta = jnp.where(jnp.logical_and(row == j, valid), meta_ref[pl.ds(at, 1), :], meta)
        out_ref[n] = jnp.concatenate(low + high + [meta], axis=0).astype(BF16)
        return c

    lax.fori_loop(0, PEERS, one_peer, 0, unroll=4)
    copies[6].wait()
    wide_ref[...] = screen_ref[...].astype(F32).reshape(128, 128)
    parts = [wide_ref[pl.ds(ri, 64, stride=2), :].reshape(8, 8, 128) for ri in range(2)]
    mine_ref[...] = jnp.concatenate(parts, axis=1).astype(BF16)


def collect_kernel(in_ref, out_ref, sem):
    core = lax.axis_index("core")
    sends = fetch([(in_ref.at[:, core], out_ref.at[x]) for x in range(4)], sem)
    for send in sends:
        send.wait()


def image_kernel(
    recv_ref, other_ref, freq_in, spread_in, xrow_in, ycol_in, i_ref, ints_out,
    freq_ref, spread_ref, xrow_ref, ycol_ref, ints_ref, meta_ref, du_ref, dv_ref, sem,
):
    pairs = ((freq_in, freq_ref), (spread_in, spread_ref), (xrow_in, xrow_ref), (ycol_in, ycol_ref))
    copies = fetch(pairs, sem)
    core = lax.axis_index("core")
    for b, block_ref in enumerate((recv_ref, other_ref)):
        for n in range(PEERS):
            meta_ref[b * PEERS + n] = block_ref[3 * n + 2].astype(F32)
    meta = meta_ref[...].reshape(512, 256).astype(BF16)
    for copy in copies:
        copy.wait()
    pick16 = lax.broadcasted_iota(jnp.int32, (16, 256), 1) % 16 == lax.broadcasted_iota(jnp.int32, (16, 256), 0)
    freq = jnp.dot(
        jnp.broadcast_to(freq_ref[...], (8, 16)),
        pick16.astype(F32),
        precision=lax.Precision.HIGHEST,
        preferred_element_type=F32,
    )[0:1]
    pick = lax.broadcasted_iota(jnp.int32, (8, 256), 0) + 96 == lax.broadcasted_iota(jnp.int32, (8, 256), 1)
    ints = lax.dot_general(
        pick.astype(F32).astype(BF16), meta, (((1,), (1,)), ((), ())), preferred_element_type=F32
    )
    ints_ref[...] = ints.astype(jnp.int32)
    send = pltpu.make_async_copy(ints_ref, ints_out, sem.at[4])
    send.start()

    def spread(k):
        return jnp.dot(meta, spread_ref[k], preferred_element_type=F32)

    du_ref[...] = (spread(0) * freq + spread(2)).reshape(2 * PEERS, 8, 256)
    dv_ref[...] = (spread(1) * freq + spread(3)).reshape(2 * PEERS, 8, 256)

    def one_slot(block_ref, row, n, j, slot):
        du = du_ref[row, j : j + 1, :]
        dv = dv_ref[row, j : j + 1, :]
        cu, su = cos_sin_turns(xrow_ref[...] * du - dv * (0.5 / SUB))
        cv, sv = cos_sin_turns(ycol_ref[...] * dv)
        left = jnp.concatenate([cu.astype(BF16), su.astype(BF16)], axis=1)
        w = block_ref[3 * n + core].astype(F32)[4 * j : 4 * j + 4, :]
        table = {}
        for p in range(2):
            re, im = w[p : p + 1, :], w[2 + p : 3 + p, :]
            for ri, (a, b) in enumerate(((re * cv, im * sv), (im * cv, re * sv))):
                minus, plus = (a - b).astype(BF16), (a + b).astype(BF16)
                table[ri, 0, p] = minus if ri == 0 else plus
                table[ri, 1, p] = plus if ri == 0 else minus
        keys = [(ri, s, p) for ri in range(2) for s in range(2) for p in range(2)]
        direct = jnp.concatenate([table[key] for key in keys], axis=0)
        turned = jnp.concatenate([-table[1, s, p] if ri == 0 else table[0, s, p] for ri, s, p in keys], axis=0)
        right = jnp.concatenate([direct, turned], axis=1)
        i_ref[slot] = lax.dot_general(left, right, (((1,), (1,)), ((), ())), preferred_element_type=F32)

    def one_peer(n, c):
        for b, block_ref in enumerate((recv_ref, other_ref)):
            for j in range(2):
                one_slot(block_ref, b * PEERS + n, n, j, 4 * n + 2 * b + j)
        return c

    lax.fori_loop(0, PEERS, one_peer, 0, unroll=2)
    send.wait()


GROUP = 32


def grid_kernel(
    ints_in, i_ref, own_ref, other_ref, taper_in, rep_in, col_in, row_in, out_ref,
    ints_ref, taper_ref, rep_ref, col_ref, row_ref, acc_ref, sem,
):
    pairs = (
        (ints_in, ints_ref), (taper_in, taper_ref), (rep_in, rep_ref), (col_in, col_ref), (row_in, row_ref),
    )
    copies = fetch(pairs, sem)
    core = lax.axis_index("core")
    acc_ref[...] = jnp.zeros(acc_ref.shape, F32)
    for copy in copies:
        copy.wait()
    taper = taper_ref[...]
    lane = lax.broadcasted_iota(jnp.int32, (8, 128), 1)
    sub = lax.broadcasted_iota(jnp.int32, (8, 128), 0)
    cell = lane % 32
    lane16 = lax.broadcasted_iota(jnp.int32, (16, 128), 1) // 32
    upper = lax.broadcasted_iota(jnp.int32, (16, 128), 0) // 8
    group_mask = [(lane16 == 2 * a + upper).astype(F32).astype(BF16) for a in range(2)]

    def station(z_core, at):
        where = ((at >> 3) * 8 + (z_core >> 1)) * 8 + (at & 7)
        mine = (z_core & 1) == core
        return jnp.where(mine, own_ref[where], other_ref[where]).astype(F32)

    def place(g, k):
        return (k // 2 % 2) * 256 + (g * (GROUP // 4) + k // 4) * 8 + k % 2

    def one_group(g, c):
        lhs_re, lhs_im = [], []
        for k in range(GROUP):
            at = place(g, k)
            sp = station(ints_ref[0, at], ints_ref[1, at])
            sq = station(ints_ref[2, at], ints_ref[3, at])
            pr, pi, qr, qi = sp[:8], sp[8:], sq[:8], sq[8:]
            gain_re = (pr * qr + pi * qi) * taper
            gain_im = (pr * qi - pi * qr) * taper
            twice_re = jnp.concatenate([gain_re, gain_re], 0).astype(BF16)
            twice_im = jnp.concatenate([gain_im, gain_im], 0).astype(BF16)
            lhs_re += [twice_re * m for m in group_mask]
            lhs_im += [twice_im * m for m in group_mask]
        wide_re = jnp.dot(jnp.concatenate(lhs_re, 0), rep_ref[0], preferred_element_type=F32)
        wide_im = jnp.dot(jnp.concatenate(lhs_im, 0), rep_ref[1], preferred_element_type=F32)
        image = i_ref[pl.ds(g * GROUP, GROUP)].reshape(GROUP * SUB, 128)
        swapped = pltpu.roll(image, 64, 1)
        corrected = (wide_re * image + wide_im * swapped).astype(BF16)
        half = jnp.dot(corrected, col_ref[...], preferred_element_type=F32).astype(BF16)
        stacked = jnp.concatenate(
            [
                jnp.concatenate([half[k * 32 : k * 32 + 32, :128], half[k * 32 : k * 32 + 32, 128:]], axis=0)
                for k in range(GROUP)
            ],
            axis=1,
        )
        cells = jnp.dot(row_ref[...], stacked, preferred_element_type=F32)
        for k in range(GROUP):
            at = place(g, k)
            row8, row_shift = ints_ref[4, at], ints_ref[5, at]
            col32, col_shift = ints_ref[6, at], ints_ref[7, at]
            keep_col = cell >= col_shift
            keep_row = sub >= row_shift
            for part in range(4):
                s = cells[part * 8 : part * 8 + 8, k * 128 : k * 128 + 128]
                near = jnp.where(keep_col, s, 0.0)
                far = s - near
                for piece, block in ((near, col32), (far, col32 + 1)):
                    if part == 0:
                        top = jnp.where(keep_row, piece, 0.0)
                        acc_ref[block, row8] += top
                        acc_ref[block, row8 + 4] += piece - top
                    else:
                        acc_ref[block, row8 + part] += piece
        return c

    lax.fori_loop(0, 2 * SLOTS // GROUP, one_group, 0)
    for band in range(16):
        for a in range(8):
            piece = acc_ref[a, 2 * band : 2 * band + 2].reshape(16, 128)
            out_ref[band, a * 16 : a * 16 + 16, :] = piece.astype(BF16)


def sum_kernel(in_ref, out_ref):
    lane = lax.broadcasted_iota(jnp.int32, (16, 128), 1) // 32
    masks = [lane == a for a in range(4)]
    for core in range(2):
        for h in range(2):
            parts = []
            for a in range(4):
                at = (h * 4 + a) * 16
                total = in_ref[core, at : at + 16, :].astype(F32)
                for z in range(1, 8):
                    total = total + in_ref[2 * z + core, at : at + 16, :].astype(F32)
                parts.append(total)
            for g in range(4):
                row = jnp.zeros((16, 128), F32)
                for a in range(4):
                    shift = (32 * (a - g)) % 128
                    moved = pltpu.roll(parts[a], shift, 1) if shift else parts[a]
                    row = jnp.where(masks[a], moved, row)
                out_ref[0, (g // 2) * 4 + 2 * core + g % 2, :, 128 * h : 128 * h + 128] = row


VM = pl.BlockSpec(memory_space=pltpu.VMEM)
SM = pl.BlockSpec(memory_space=pltpu.SMEM)
HBM = pl.BlockSpec(memory_space=pltpu.HBM)
call = functools.partial(
    pl.pallas_call, compiler_params=pltpu.CompilerParams(vmem_limit_bytes=16 << 20)
)


def pinned(x):
    return pltpu.with_memory_space_constraint(x, pltpu.HBM)


def pack(*args):
    return call(
        pack_kernel,
        out_shape=(
            jax.ShapeDtypeStruct((PEERS, 24, 256), BF16),
            jax.ShapeDtypeStruct((8, 16, 128), BF16),
        ),
        in_specs=[HBM] * 7,
        out_specs=(VM, VM),
        scratch_shapes=[pltpu.SMEM(args[0].shape, jnp.int32)]
        + [pltpu.VMEM(a.shape, a.dtype) for a in args[1:6]]
        + [
            pltpu.VMEM((8, 16, 128), BF16),
            pltpu.VMEM((32, 256), F32),
            pltpu.VMEM((128, 128), F32),
            pltpu.SMEM((SLOTS,), jnp.int32),
            pltpu.SMEM((PEERS,), jnp.int32),
            pltpu.SemaphoreType.DMA((8,)),
        ],
        name="pack",
    )(*[pinned(a) for a in args])


def collect(quarter):
    return call(
        collect_kernel,
        out_shape=jax.ShapeDtypeStruct((4, 8, 8, 16, 128), BF16),
        in_specs=[VM],
        out_specs=HBM,
        scratch_shapes=[pltpu.SemaphoreType.DMA((4,))],
        name="collect",
    )(quarter)


def images(recv, sibling, freq):
    xrow = np.broadcast_to(((ROW_L - 16.0) / SUB)[:, None], (SUB, 256)).astype(np.float32)
    ycol = np.broadcast_to(((np.arange(16) + 0.5) / SUB)[:, None], (16, 256)).astype(np.float32)
    args = (freq, jnp.asarray(spread_tables(), BF16), jnp.asarray(xrow), jnp.asarray(ycol))
    return call(
        image_kernel,
        out_shape=(
            jax.ShapeDtypeStruct((2 * SLOTS, SUB, 128), F32),
            jax.ShapeDtypeStruct((8, 512), jnp.int32),
        ),
        in_specs=[VM, VM] + [HBM] * 4,
        out_specs=(VM, HBM),
        scratch_shapes=[pltpu.VMEM(a.shape, a.dtype) for a in args]
        + [pltpu.VMEM((8, 512), jnp.int32)]
        + [pltpu.VMEM((2 * PEERS, 8, 256), F32)] * 3
        + [pltpu.SemaphoreType.DMA((5,))],
        name="images",
    )(recv, sibling, *[pinned(a) for a in args])


def grid_tile(ints, image, own, other):
    tables = (
        jnp.asarray(taper_table()),
        jnp.asarray(replicate_tables(), BF16),
        jnp.asarray(column_table(), BF16),
        jnp.asarray(row_table(), BF16),
    )
    return call(
        grid_kernel,
        out_shape=jax.ShapeDtypeStruct((16, 128, 128), BF16),
        in_specs=[HBM, VM, VM, VM] + [HBM] * 4,
        out_specs=VM,
        scratch_shapes=[pltpu.SMEM(ints.shape, jnp.int32)]
        + [pltpu.VMEM(t.shape, t.dtype) for t in tables]
        + [pltpu.VMEM((9, 33, 8, 128), F32), pltpu.SemaphoreType.DMA((5,))],
        name="grid_tile",
    )(pinned(ints), image, own, other, *[pinned(t) for t in tables])


def band_sum(arrived):
    return call(
        sum_kernel,
        out_shape=jax.ShapeDtypeStruct((1, 8, 16, 256), F32),
        in_specs=[VM],
        out_specs=VM,
        name="band_sum",
    )(arrived)


SWAP = [(0, 1), (1, 0)]


def on_device(visibilities, weights, uv_coords, freq_ratio, screens, stations, offsets, tile_ids):
    uv = jnp.transpose(uv_coords, (1, 2, 0)).reshape(32, 32)
    pairs = jnp.transpose(screens.reshape(32, 2, 8, 128), (0, 2, 1, 3)).reshape(32, 16, 128)
    packed, mine = pack(tile_ids.T, visibilities, weights, uv, stations.T, offsets.T, pairs)
    recv = lax.all_to_all(packed, ("x", "y"), split_axis=0, concat_axis=0, tiled=True)
    quarter = lax.all_gather(mine, ("z", "core"), axis=0, tiled=True).reshape(8, 2, 8, 16, 128)
    own = lax.all_to_all(collect(quarter), "x", split_axis=0, concat_axis=0, tiled=True).reshape(256, 16, 128)
    sibling = lax.ppermute(recv, "core", SWAP)
    image, ints = images(recv.reshape(96, 8, 256), sibling.reshape(96, 8, 256), freq_ratio[None, :])
    own, image = lax.optimization_barrier((own, image))
    other = lax.ppermute(own, "core", SWAP)
    partial = grid_tile(ints, image, own, other)
    arrived = lax.all_to_all(partial, ("z", "core"), split_axis=0, concat_axis=0, tiled=True)
    return band_sum(arrived)


def solution(mesh):
    stat, tile = mesh.shape["stat"], mesh.shape["tile"]
    every = ("z", "core", "x", "y")
    fine = Mesh(mesh.devices.reshape(stat // 2, 2, 4, tile // 4), every)
    placed = (
        P(every, None, None),
        P(every, None),
        P(every, None, None),
        P(),
        P(("z", "core"), None, None),
        P(every, None),
        P(every, None),
        P(every, None),
    )
    return jax.shard_map(
        on_device,
        mesh=fine,
        in_specs=placed,
        out_specs=P(("x", "y"), None, ("z", "core"), None),
        check_vma=False,
    )
```

```python
import functools
import math

import jax
import jax.numpy as jnp
import numpy as np
from jax import lax
from jax.experimental import pallas as pl
from jax.experimental.pallas import tpu as pltpu
from jax.sharding import Mesh, PartitionSpec as P

SUB = 32
TS = 256
K = 256
SLOTS = 64
PEERS = 32
F32 = jnp.float32
BF16 = jnp.bfloat16

ROW_L = np.array([4 * (r % 8) + r // 8 for r in range(SUB)])
LANE = np.arange(128)
LANE_I = LANE % 16
LANE_P = (LANE // 16) % 2
LANE_RI = LANE // 64
LANE_M = np.where((LANE // 32) % 2 == 0, 16 + LANE_I, 15 - LANE_I)


def spread_tables():
    out = np.zeros((4, 256, 256), np.float32)
    for part in range(3):
        for t in range(16):
            out[0, part * 32 + t, t * 16 : (t + 1) * 16] = 1.0
            out[1, part * 32 + 16 + t, t * 16 : (t + 1) * 16] = 1.0
    out[2, 101, :] = 1.0
    out[3, 103, :] = 1.0
    return out


def replicate_tables():
    cell = np.arange(128) % 32
    rep = (cell[:, None] == LANE_M[None, :]).astype(np.float32)
    sign = np.where(LANE_RI == 0, -1.0, 1.0).astype(np.float32)
    return np.stack([rep, rep * sign[None, :]])


def column_table():
    n = np.arange(256)
    twice, ri, p, v = n // 128, (n // 64) % 2, (n // 32) % 2, n % 32
    turns = -(LANE_M[:, None] - 16.0) * (v[None, :] - 16.0) / SUB
    turns = turns + 0.25 * (twice[None, :] - ri[None, :] + LANE_RI[:, None])
    val = np.cos(2.0 * np.pi * turns)
    return np.where(LANE_P[:, None] == p[None, :], val, 0.0)


def row_table():
    u, part, l = np.arange(32), np.arange(64) // 32, ROW_L[np.arange(64) % 32]
    angle = -2.0 * np.pi / SUB * (u[:, None] - 16.0) * (l[None, :] - 16.0)
    return np.where(part[None, :] == 0, np.cos(angle), np.sin(angle))


def taper_table():
    flat = np.arange(1024)
    l, m = flat // 32, flat % 32
    one = np.sin(np.pi * (np.arange(SUB) + 0.5) / SUB)
    return (one[l] * one[m] / (K * SUB)).reshape(8, 128).astype(np.float32)


def fit_turns():
    s = (0.5 * np.cos(np.pi * (np.arange(400) + 0.5) / 800)) ** 2
    r = np.sqrt(s)
    cheb = np.polynomial.chebyshev.Chebyshev.fit
    cos = cheb(s, np.cos(2 * np.pi * r), 5, domain=[0, 0.25]).convert(kind=np.polynomial.Polynomial)
    sin = cheb(s, np.sin(2 * np.pi * r) / r, 5, domain=[0, 0.25]).convert(kind=np.polynomial.Polynomial)
    return [float(c) for c in cos.coef], [float(c) for c in sin.coef]


COS_C, SIN_C = fit_turns()


def horner(coef, s):
    acc = jnp.full_like(s, coef[-1])
    for c in coef[-2::-1]:
        acc = acc * s + c
    return acc


def cos_sin_turns(turns):
    r = turns - jnp.round(turns)
    s = r * r
    return horner(COS_C, s), horner(SIN_C, s) * r


def fetch(pairs, sem):
    copies = [pltpu.make_async_copy(src, dst, sem.at[i]) for i, (src, dst) in enumerate(pairs)]
    for copy in copies:
        copy.start()
    return copies


def pack_kernel(
    tile_in, vis_in, weight_in, uv_in, station_in, offset_in, screen_in, out_ref, mine_ref,
    tile_ref, vis_ref, weight_ref, uv_ref, station_ref, offset_ref, screen_ref,
    meta_ref, wide_ref, src_ref, count_ref, sem,
):
    pairs = (
        (tile_in, tile_ref), (station_in, station_ref), (offset_in, offset_ref),
        (uv_in, uv_ref), (weight_in, weight_ref), (vis_in, vis_ref), (screen_in.at[pl.ds(8 * (2 * lax.axis_index("xl") + lax.axis_index("yl")), 8)], screen_ref),
    )
    copies = fetch(pairs, sem)
    for copy in copies[:4]:
        copy.wait()
    uv = uv_ref[...]
    hi = uv.astype(BF16)
    rest = uv - hi.astype(F32)
    mid = rest.astype(BF16)
    low = (rest - mid.astype(F32)).astype(BF16)
    p, q = station_ref[0:1, :], station_ref[1:2, :]
    r, c = offset_ref[0:1, :], offset_ref[1:2, :]
    ints = jnp.concatenate([p >> 5, p & 31, q >> 5, q & 31, r >> 3, r & 7, c >> 5, c & 31], axis=0)
    columns = jnp.concatenate([hi.astype(F32), mid.astype(F32), low.astype(F32), ints.astype(F32)], axis=0)
    eye = lax.broadcasted_iota(jnp.int32, (104, 256), 0) == lax.broadcasted_iota(jnp.int32, (104, 256), 1)
    meta_ref[...] = lax.dot_general(
        columns.astype(BF16),
        eye.astype(F32).astype(BF16),
        (((0,), (0,)), ((), ())),
        preferred_element_type=F32,
    )

    def clear(i, c):
        src_ref[2 * i] = -1
        src_ref[2 * i + 1] = -1
        count_ref[i] = 0
        return c

    lax.fori_loop(0, PEERS, clear, 0, unroll=8)

    def assign(s, c):
        t = tile_ref[0, s]
        before = count_ref[t]
        src_ref[2 * t + before] = s
        count_ref[t] = before + 1
        return c

    lax.fori_loop(0, 32, assign, 0, unroll=4)
    row = lax.broadcasted_iota(jnp.int32, (8, 256), 0)
    for copy in copies[4:6]:
        copy.wait()

    def one_peer(n, c):
        low, high = [], []
        meta = jnp.zeros((8, 256), F32)
        for j in range(2):
            s = src_ref[2 * n + j]
            valid = s >= 0
            at = jnp.maximum(s, 0)
            weighted = jnp.where(valid, vis_ref[at] * weight_ref[pl.ds(at, 1), :], 0.0)
            low += [weighted[0:2], weighted[4:6]]
            high += [weighted[2:4], weighted[6:8]]
            meta = jnp.where(jnp.logical_and(row == j, valid), meta_ref[pl.ds(at, 1), :], meta)
        out_ref[n] = jnp.concatenate(low + high + [meta], axis=0).astype(BF16)
        return c

    lax.fori_loop(0, PEERS, one_peer, 0, unroll=4)
    copies[6].wait()
    wide_ref[...] = screen_ref[...].astype(F32).reshape(128, 128)
    parts = [wide_ref[pl.ds(ri, 64, stride=2), :].reshape(8, 8, 128) for ri in range(2)]
    mine_ref[...] = jnp.concatenate(parts, axis=1).astype(BF16)


def collect_kernel(in_ref, out_ref):
    core = lax.axis_index("core")
    for z in range(8):
        piece = in_ref[z, core]
        for x in range(4):
            out_ref[x, z] = piece


def image_kernel(
    recv_ref, other_ref, freq_in, spread_in, xrow_in, ycol_in, i_ref, ints_out,
    freq_ref, spread_ref, xrow_ref, ycol_ref, ints_ref, meta_ref, du_ref, dv_ref, sem,
):
    pairs = ((freq_in, freq_ref), (spread_in, spread_ref), (xrow_in, xrow_ref), (ycol_in, ycol_ref))
    copies = fetch(pairs, sem)
    core = lax.axis_index("core")
    for b, block_ref in enumerate((recv_ref, other_ref)):
        for n in range(PEERS):
            meta_ref[b * PEERS + n] = block_ref[3 * n + 2].astype(F32)
    meta = meta_ref[...].reshape(512, 256).astype(BF16)
    for copy in copies:
        copy.wait()
    pick16 = lax.broadcasted_iota(jnp.int32, (16, 256), 1) % 16 == lax.broadcasted_iota(jnp.int32, (16, 256), 0)
    freq = jnp.dot(
        jnp.broadcast_to(freq_ref[...], (8, 16)),
        pick16.astype(F32),
        precision=lax.Precision.HIGHEST,
        preferred_element_type=F32,
    )[0:1]
    pick = lax.broadcasted_iota(jnp.int32, (8, 256), 0) + 96 == lax.broadcasted_iota(jnp.int32, (8, 256), 1)
    ints = lax.dot_general(
        pick.astype(F32).astype(BF16), meta, (((1,), (1,)), ((), ())), preferred_element_type=F32
    )
    ints_ref[...] = ints.astype(jnp.int32)
    send = pltpu.make_async_copy(ints_ref, ints_out, sem.at[4])
    send.start()

    def spread(k):
        return jnp.dot(meta, spread_ref[k], preferred_element_type=F32)

    du_ref[...] = (spread(0) * freq + spread(2)).reshape(2 * PEERS, 8, 256)
    dv_ref[...] = (spread(1) * freq + spread(3)).reshape(2 * PEERS, 8, 256)

    def one_slot(block_ref, row, n, j, slot):
        du = du_ref[row, j : j + 1, :]
        dv = dv_ref[row, j : j + 1, :]
        cu, su = cos_sin_turns(xrow_ref[...] * du - dv * (0.5 / SUB))
        cv, sv = cos_sin_turns(ycol_ref[...] * dv)
        left = jnp.concatenate([cu.astype(BF16), su.astype(BF16)], axis=1)
        w = block_ref[3 * n + core].astype(F32)[4 * j : 4 * j + 4, :]
        table = {}
        for p in range(2):
            re, im = w[p : p + 1, :], w[2 + p : 3 + p, :]
            for ri, (a, b) in enumerate(((re * cv, im * sv), (im * cv, re * sv))):
                minus, plus = (a - b).astype(BF16), (a + b).astype(BF16)
                table[ri, 0, p] = minus if ri == 0 else plus
                table[ri, 1, p] = plus if ri == 0 else minus
        keys = [(ri, s, p) for ri in range(2) for s in range(2) for p in range(2)]
        direct = jnp.concatenate([table[key] for key in keys], axis=0)
        turned = jnp.concatenate([-table[1, s, p] if ri == 0 else table[0, s, p] for ri, s, p in keys], axis=0)
        right = jnp.concatenate([direct, turned], axis=1)
        i_ref[slot] = lax.dot_general(left, right, (((1,), (1,)), ((), ())), preferred_element_type=F32)

    def one_peer(n, c):
        for b, block_ref in enumerate((recv_ref, other_ref)):
            for j in range(2):
                one_slot(block_ref, b * PEERS + n, n, j, 4 * n + 2 * b + j)
        return c

    lax.fori_loop(0, PEERS, one_peer, 0, unroll=4)
    send.wait()


GROUP = 64


def grid_kernel(
    ints_in, i_ref, own_ref, other_ref, taper_in, rep_in, col_in, row_in, out_ref,
    ints_ref, taper_ref, rep_ref, col_ref, row_ref, acc_ref, sem,
):
    pairs = (
        (ints_in, ints_ref), (taper_in, taper_ref), (rep_in, rep_ref), (col_in, col_ref), (row_in, row_ref),
    )
    copies = fetch(pairs, sem)
    core = lax.axis_index("core")
    acc_ref[...] = jnp.zeros(acc_ref.shape, F32)
    for copy in copies:
        copy.wait()
    taper = taper_ref[...]
    lane = lax.broadcasted_iota(jnp.int32, (8, 128), 1)
    sub = lax.broadcasted_iota(jnp.int32, (8, 128), 0)
    cell = lane % 32
    lane16 = lax.broadcasted_iota(jnp.int32, (16, 128), 1) // 32
    upper = lax.broadcasted_iota(jnp.int32, (16, 128), 0) // 8
    group_mask = [(lane16 == 2 * a + upper).astype(F32).astype(BF16) for a in range(2)]

    def station(z_core, at):
        where = ((at >> 3) * 8 + (z_core >> 1)) * 8 + (at & 7)
        mine = (z_core & 1) == core
        return jnp.where(mine, own_ref[where], other_ref[where]).astype(F32)

    def place(g, k):
        return (k // 2 % 2) * 256 + (g * (GROUP // 4) + k // 4) * 8 + k % 2

    def one_group(g, c):
        lhs_re, lhs_im = [], []
        for k in range(GROUP):
            at = place(g, k)
            sp = station(ints_ref[0, at], ints_ref[1, at])
            sq = station(ints_ref[2, at], ints_ref[3, at])
            pr, pi, qr, qi = sp[:8], sp[8:], sq[:8], sq[8:]
            gain_re = (pr * qr + pi * qi) * taper
            gain_im = (pr * qi - pi * qr) * taper
            twice_re = jnp.concatenate([gain_re, gain_re], 0).astype(BF16)
            twice_im = jnp.concatenate([gain_im, gain_im], 0).astype(BF16)
            lhs_re += [twice_re * m for m in group_mask]
            lhs_im += [twice_im * m for m in group_mask]
        wide_re = jnp.dot(jnp.concatenate(lhs_re, 0), rep_ref[0], preferred_element_type=F32)
        wide_im = jnp.dot(jnp.concatenate(lhs_im, 0), rep_ref[1], preferred_element_type=F32)
        image = i_ref[pl.ds(g * GROUP, GROUP)].reshape(GROUP * SUB, 128)
        swapped = pltpu.roll(image, 64, 1)
        corrected = (wide_re * image + wide_im * swapped).astype(BF16)
        half = jnp.dot(corrected, col_ref[...], preferred_element_type=F32).astype(BF16)
        stacked = jnp.concatenate(
            [
                jnp.concatenate([half[k * 32 : k * 32 + 32, :128], half[k * 32 : k * 32 + 32, 128:]], axis=0)
                for k in range(GROUP)
            ],
            axis=1,
        )
        cells = jnp.dot(row_ref[...], stacked, preferred_element_type=F32)
        for k in range(GROUP):
            at = place(g, k)
            row8, row_shift = ints_ref[4, at], ints_ref[5, at]
            col32, col_shift = ints_ref[6, at], ints_ref[7, at]
            keep_col = cell >= col_shift
            keep_row = sub >= row_shift
            for part in range(4):
                s = cells[part * 8 : part * 8 + 8, k * 128 : k * 128 + 128]
                near = jnp.where(keep_col, s, 0.0)
                far = s - near
                for piece, block in ((near, col32), (far, col32 + 1)):
                    if part == 0:
                        top = jnp.where(keep_row, piece, 0.0)
                        acc_ref[block, row8] += top
                        acc_ref[block, row8 + 4] += piece - top
                    else:
                        acc_ref[block, row8 + part] += piece
        return c

    lax.fori_loop(0, 2 * SLOTS // GROUP, one_group, 0)
    for band in range(16):
        for a in range(8):
            piece = acc_ref[a, 2 * band : 2 * band + 2].reshape(16, 128)
            out_ref[band, a * 16 : a * 16 + 16, :] = piece.astype(BF16)


def sum_kernel(in_ref, out_ref):
    lane = lax.broadcasted_iota(jnp.int32, (16, 128), 1) // 32
    masks = [lane == a for a in range(4)]
    for core in range(2):
        for h in range(2):
            parts = []
            for a in range(4):
                at = (h * 4 + a) * 16
                total = in_ref[core, at : at + 16, :].astype(F32)
                for z in range(1, 8):
                    total = total + in_ref[2 * z + core, at : at + 16, :].astype(F32)
                parts.append(total)
            for g in range(4):
                row = jnp.zeros((16, 128), F32)
                for a in range(4):
                    shift = (32 * (a - g)) % 128
                    moved = pltpu.roll(parts[a], shift, 1) if shift else parts[a]
                    row = jnp.where(masks[a], moved, row)
                out_ref[0, (g // 2) * 4 + 2 * core + g % 2, :, 128 * h : 128 * h + 128] = row


VM = pl.BlockSpec(memory_space=pltpu.VMEM)
SM = pl.BlockSpec(memory_space=pltpu.SMEM)
HBM = pl.BlockSpec(memory_space=pltpu.HBM)
call = functools.partial(
    pl.pallas_call, compiler_params=pltpu.CompilerParams(vmem_limit_bytes=16 << 20)
)


def pinned(x):
    return pltpu.with_memory_space_constraint(x, pltpu.HBM)


def pack(*args):
    return call(
        pack_kernel,
        out_shape=(
            jax.ShapeDtypeStruct((PEERS, 24, 256), BF16),
            jax.ShapeDtypeStruct((8, 16, 128), BF16),
        ),
        in_specs=[HBM] * 7,
        out_specs=(VM, VM),
        scratch_shapes=[pltpu.SMEM(args[0].shape, jnp.int32)]
        + [pltpu.VMEM(a.shape, a.dtype) for a in args[1:6]]
        + [
            pltpu.VMEM((8, 16, 128), BF16),
            pltpu.VMEM((32, 256), F32),
            pltpu.VMEM((128, 128), F32),
            pltpu.SMEM((SLOTS,), jnp.int32),
            pltpu.SMEM((PEERS,), jnp.int32),
            pltpu.SemaphoreType.DMA((8,)),
        ],
        name="pack",
    )(*[pinned(a) for a in args])


def collect(quarter):
    return call(
        collect_kernel,
        out_shape=jax.ShapeDtypeStruct((4, 8, 8, 16, 128), BF16),
        in_specs=[VM],
        out_specs=VM,
        name="collect",
    )(quarter)


def images(recv, sibling, freq):
    xrow = np.broadcast_to(((ROW_L - 16.0) / SUB)[:, None], (SUB, 256)).astype(np.float32)
    ycol = np.broadcast_to(((np.arange(16) + 0.5) / SUB)[:, None], (16, 256)).astype(np.float32)
    args = (freq, jnp.asarray(spread_tables(), BF16), jnp.asarray(xrow), jnp.asarray(ycol))
    return call(
        image_kernel,
        out_shape=(
            jax.ShapeDtypeStruct((2 * SLOTS, SUB, 128), F32),
            jax.ShapeDtypeStruct((8, 512), jnp.int32),
        ),
        in_specs=[VM, VM] + [HBM] * 4,
        out_specs=(VM, HBM),
        scratch_shapes=[pltpu.VMEM(a.shape, a.dtype) for a in args]
        + [pltpu.VMEM((8, 512), jnp.int32)]
        + [pltpu.VMEM((2 * PEERS, 8, 256), F32)] * 3
        + [pltpu.SemaphoreType.DMA((5,))],
        name="images",
    )(recv, sibling, *[pinned(a) for a in args])


def grid_tile(ints, image, own, other):
    tables = (
        jnp.asarray(taper_table()),
        jnp.asarray(replicate_tables(), BF16),
        jnp.asarray(column_table(), BF16),
        jnp.asarray(row_table(), BF16),
    )
    return call(
        grid_kernel,
        out_shape=jax.ShapeDtypeStruct((16, 128, 128), BF16),
        in_specs=[HBM, VM, VM, VM] + [HBM] * 4,
        out_specs=VM,
        scratch_shapes=[pltpu.SMEM(ints.shape, jnp.int32)]
        + [pltpu.VMEM(t.shape, t.dtype) for t in tables]
        + [pltpu.VMEM((9, 33, 8, 128), F32), pltpu.SemaphoreType.DMA((5,))],
        name="grid_tile",
    )(pinned(ints), image, own, other, *[pinned(t) for t in tables])


def band_sum(arrived):
    return call(
        sum_kernel,
        out_shape=jax.ShapeDtypeStruct((1, 8, 16, 256), F32),
        in_specs=[VM],
        out_specs=VM,
        name="band_sum",
    )(arrived)


SWAP = [(0, 1), (1, 0)]


def on_device(visibilities, weights, uv_coords, freq_ratio, screens, stations, offsets, tile_ids):
    uv = jnp.transpose(uv_coords, (1, 2, 0)).reshape(32, 32)
    pairs = jnp.transpose(screens.reshape(32, 2, 8, 128), (0, 2, 1, 3)).reshape(32, 16, 128)
    packed, mine = pack(tile_ids.T, visibilities, weights, uv, stations.T, offsets.T, pairs)
    recv = lax.all_to_all(packed, ("xh", "xl", "yh", "yl"), split_axis=0, concat_axis=0, tiled=True)
    quarter = lax.all_gather(mine, ("z", "core"), axis=0, tiled=True).reshape(8, 2, 8, 16, 128)
    own = lax.all_to_all(collect(quarter), ("xl", "yl"), split_axis=0, concat_axis=0, tiled=True).reshape(256, 16, 128)
    sibling = lax.ppermute(recv, "core", SWAP)
    image, ints = images(recv.reshape(96, 8, 256), sibling.reshape(96, 8, 256), freq_ratio[None, :])
    own, image = lax.optimization_barrier((own, image))
    other = lax.ppermute(own, "core", SWAP)
    partial = grid_tile(ints, image, own, other)
    arrived = lax.all_to_all(partial, ("z", "core"), split_axis=0, concat_axis=0, tiled=True)
    return band_sum(arrived)


def solution(mesh):
    stat, tile = mesh.shape["stat"], mesh.shape["tile"]
    every = ("z", "core", "xh", "xl", "yh", "yl")
    fine = Mesh(mesh.devices.reshape(stat // 2, 2, 2, 2, tile // 8, 2), every)
    placed = (
        P(every, None, None),
        P(every, None),
        P(every, None, None),
        P(),
        P(("z", "core"), None, None),
        P(every, None),
        P(every, None),
        P(every, None),
    )
    return jax.shard_map(
        on_device,
        mesh=fine,
        in_specs=placed,
        out_specs=P(("xh", "xl", "yh", "yl"), None, ("z", "core"), None),
        check_vma=False,
    )
```

```python
import functools
import math

import jax
import jax.numpy as jnp
import numpy as np
from jax import lax
from jax.experimental import pallas as pl
from jax.experimental.pallas import tpu as pltpu
from jax.sharding import Mesh, PartitionSpec as P

SUB = 32
TS = 256
K = 256
SLOTS = 64
PEERS = 32
F32 = jnp.float32
BF16 = jnp.bfloat16

ROW_L = np.array([4 * (r % 8) + r // 8 for r in range(SUB)])
LANE = np.arange(128)
LANE_I = LANE % 16
LANE_P = (LANE // 16) % 2
LANE_RI = LANE // 64
LANE_M = np.where((LANE // 32) % 2 == 0, 16 + LANE_I, 15 - LANE_I)


def spread_tables():
    out = np.zeros((4, 256, 256), np.float32)
    for part in range(3):
        for t in range(16):
            out[0, part * 32 + t, t * 16 : (t + 1) * 16] = 1.0
            out[1, part * 32 + 16 + t, t * 16 : (t + 1) * 16] = 1.0
    out[2, 101, :] = 1.0
    out[3, 103, :] = 1.0
    return out


def replicate_tables():
    cell = np.arange(128) % 32
    rep = (cell[:, None] == LANE_M[None, :]).astype(np.float32)
    sign = np.where(LANE_RI == 0, -1.0, 1.0).astype(np.float32)
    return np.stack([rep, rep * sign[None, :]])


def column_table():
    n = np.arange(256)
    twice, ri, p, v = n // 128, (n // 64) % 2, (n // 32) % 2, n % 32
    turns = -(LANE_M[:, None] - 16.0) * (v[None, :] - 16.0) / SUB
    turns = turns + 0.25 * (twice[None, :] - ri[None, :] + LANE_RI[:, None])
    val = np.cos(2.0 * np.pi * turns)
    return np.where(LANE_P[:, None] == p[None, :], val, 0.0)


def row_table():
    u, part, l = np.arange(32), np.arange(64) // 32, ROW_L[np.arange(64) % 32]
    angle = -2.0 * np.pi / SUB * (u[:, None] - 16.0) * (l[None, :] - 16.0)
    return np.where(part[None, :] == 0, np.cos(angle), np.sin(angle))


def taper_table():
    flat = np.arange(1024)
    l, m = flat // 32, flat % 32
    one = np.sin(np.pi * (np.arange(SUB) + 0.5) / SUB)
    return (one[l] * one[m] / (K * SUB)).reshape(8, 128).astype(np.float32)


def fit_turns():
    s = (0.5 * np.cos(np.pi * (np.arange(400) + 0.5) / 800)) ** 2
    r = np.sqrt(s)
    cheb = np.polynomial.chebyshev.Chebyshev.fit
    cos = cheb(s, np.cos(2 * np.pi * r), 5, domain=[0, 0.25]).convert(kind=np.polynomial.Polynomial)
    sin = cheb(s, np.sin(2 * np.pi * r) / r, 5, domain=[0, 0.25]).convert(kind=np.polynomial.Polynomial)
    return [float(c) for c in cos.coef], [float(c) for c in sin.coef]


COS_C, SIN_C = fit_turns()


def horner(coef, s):
    acc = jnp.full_like(s, coef[-1])
    for c in coef[-2::-1]:
        acc = acc * s + c
    return acc


def cos_sin_turns(turns):
    r = turns - jnp.round(turns)
    s = r * r
    return horner(COS_C, s), horner(SIN_C, s) * r


def fetch(pairs, sem):
    copies = [pltpu.make_async_copy(src, dst, sem.at[i]) for i, (src, dst) in enumerate(pairs)]
    for copy in copies:
        copy.start()
    return copies


def pack_kernel(
    tile_in, vis_in, weight_in, uv_in, station_in, offset_in, screen_in, out_ref, mine_ref,
    tile_ref, vis_ref, weight_ref, uv_ref, station_ref, offset_ref, screen_ref,
    meta_ref, wide_ref, src_ref, count_ref, sem,
):
    pairs = (
        (tile_in, tile_ref), (station_in, station_ref), (offset_in, offset_ref),
        (uv_in, uv_ref), (weight_in, weight_ref), (vis_in, vis_ref), (screen_in.at[pl.ds(8 * (2 * lax.axis_index("xl") + lax.axis_index("yl")), 8)], screen_ref),
    )
    copies = fetch(pairs, sem)

    def clear(i, c):
        src_ref[2 * i] = -1
        src_ref[2 * i + 1] = -1
        count_ref[i] = 0
        return c

    lax.fori_loop(0, PEERS, clear, 0, unroll=8)

    copies[0].wait()

    def assign(s, c):
        t = tile_ref[0, s]
        before = count_ref[t]
        src_ref[2 * t + before] = s
        count_ref[t] = before + 1
        return c

    lax.fori_loop(0, 32, assign, 0, unroll=4)
    for copy in copies[1:4]:
        copy.wait()
    uv = uv_ref[...]
    hi = uv.astype(BF16)
    rest = uv - hi.astype(F32)
    mid = rest.astype(BF16)
    low = (rest - mid.astype(F32)).astype(BF16)
    p, q = station_ref[0:1, :], station_ref[1:2, :]
    r, c = offset_ref[0:1, :], offset_ref[1:2, :]
    ints = jnp.concatenate([p >> 5, p & 31, q >> 5, q & 31, r >> 3, r & 7, c >> 5, c & 31], axis=0)
    columns = jnp.concatenate([hi.astype(F32), mid.astype(F32), low.astype(F32), ints.astype(F32)], axis=0)
    eye = lax.broadcasted_iota(jnp.int32, (104, 256), 0) == lax.broadcasted_iota(jnp.int32, (104, 256), 1)
    meta_ref[...] = lax.dot_general(
        columns.astype(BF16),
        eye.astype(F32).astype(BF16),
        (((0,), (0,)), ((), ())),
        preferred_element_type=F32,
    )

    row = lax.broadcasted_iota(jnp.int32, (8, 256), 0)
    for copy in copies[4:6]:
        copy.wait()

    def one_peer(n, c):
        low, high = [], []
        meta = jnp.zeros((8, 256), F32)
        for j in range(2):
            s = src_ref[2 * n + j]
            valid = s >= 0
            at = jnp.maximum(s, 0)
            weighted = jnp.where(valid, vis_ref[at] * weight_ref[pl.ds(at, 1), :], 0.0)
            low += [weighted[0:2], weighted[4:6]]
            high += [weighted[2:4], weighted[6:8]]
            meta = jnp.where(jnp.logical_and(row == j, valid), meta_ref[pl.ds(at, 1), :], meta)
        out_ref[n] = jnp.concatenate(low + high + [meta], axis=0).astype(BF16)
        return c

    lax.fori_loop(0, PEERS, one_peer, 0, unroll=16)
    copies[6].wait()
    wide_ref[...] = screen_ref[...].astype(F32).reshape(128, 128)
    parts = [wide_ref[pl.ds(ri, 64, stride=2), :].reshape(8, 8, 128) for ri in range(2)]
    mine_ref[...] = jnp.concatenate(parts, axis=1).astype(BF16)


def collect_kernel(in_ref, out_ref):
    core = lax.axis_index("core")
    for z in range(8):
        piece = in_ref[z, core]
        for x in range(4):
            out_ref[x, z] = piece


def image_kernel(
    recv_ref, other_ref, freq_in, spread_in, xrow_in, ycol_in, i_ref, ints_out,
    freq_ref, spread_ref, xrow_ref, ycol_ref, ints_ref, meta_ref, du_ref, dv_ref, sem,
):
    pairs = ((freq_in, freq_ref), (spread_in, spread_ref), (xrow_in, xrow_ref), (ycol_in, ycol_ref))
    copies = fetch(pairs, sem)
    core = lax.axis_index("core")
    for b, block_ref in enumerate((recv_ref, other_ref)):
        for n in range(PEERS):
            meta_ref[b * PEERS + n] = block_ref[3 * n + 2].astype(F32)
    meta = meta_ref[...].reshape(512, 256).astype(BF16)
    for copy in copies:
        copy.wait()
    pick16 = lax.broadcasted_iota(jnp.int32, (16, 256), 1) % 16 == lax.broadcasted_iota(jnp.int32, (16, 256), 0)
    freq = jnp.dot(
        jnp.broadcast_to(freq_ref[...], (8, 16)),
        pick16.astype(F32),
        precision=lax.Precision.HIGHEST,
        preferred_element_type=F32,
    )[0:1]
    pick = lax.broadcasted_iota(jnp.int32, (8, 256), 0) + 96 == lax.broadcasted_iota(jnp.int32, (8, 256), 1)
    ints = lax.dot_general(
        pick.astype(F32).astype(BF16), meta, (((1,), (1,)), ((), ())), preferred_element_type=F32
    )
    row = lax.broadcasted_iota(jnp.int32, (512, 128), 0)
    slot = jnp.where(row & 7 < 2, ((row >> 3) & 31) * 4 + (row >> 8) * 2 + (row & 7), -1)
    chosen = (slot == lax.broadcasted_iota(jnp.int32, (512, 128), 1)).astype(F32).astype(BF16)
    ints_ref[...] = jnp.dot(ints.astype(BF16), chosen, preferred_element_type=F32).astype(jnp.int32)
    send = pltpu.make_async_copy(ints_ref, ints_out, sem.at[4])
    send.start()

    def spread(k):
        return jnp.dot(meta, spread_ref[k], preferred_element_type=F32)

    du_ref[...] = (spread(0) * freq + spread(2)).reshape(2 * PEERS, 8, 256)
    dv_ref[...] = (spread(1) * freq + spread(3)).reshape(2 * PEERS, 8, 256)

    def one_slot(block_ref, row, n, j, slot):
        du = du_ref[row, j : j + 1, :]
        dv = dv_ref[row, j : j + 1, :]
        cu, su = cos_sin_turns(xrow_ref[...] * du - dv * (0.5 / SUB))
        cv, sv = cos_sin_turns(ycol_ref[...] * dv)
        left = jnp.concatenate([cu.astype(BF16), su.astype(BF16)], axis=1)
        w = block_ref[3 * n + core].astype(F32)[4 * j : 4 * j + 4, :]
        table = {}
        for p in range(2):
            re, im = w[p : p + 1, :], w[2 + p : 3 + p, :]
            for ri, (a, b) in enumerate(((re * cv, im * sv), (im * cv, re * sv))):
                minus, plus = (a - b).astype(BF16), (a + b).astype(BF16)
                table[ri, 0, p] = minus if ri == 0 else plus
                table[ri, 1, p] = plus if ri == 0 else minus
        keys = [(ri, s, p) for ri in range(2) for s in range(2) for p in range(2)]
        direct = jnp.concatenate([table[key] for key in keys], axis=0)
        turned = jnp.concatenate([-table[1, s, p] if ri == 0 else table[0, s, p] for ri, s, p in keys], axis=0)
        right = jnp.concatenate([direct, turned], axis=1)
        i_ref[slot] = lax.dot_general(left, right, (((1,), (1,)), ((), ())), preferred_element_type=F32)

    def one_peer(n, c):
        for b, block_ref in enumerate((recv_ref, other_ref)):
            for j in range(2):
                one_slot(block_ref, b * PEERS + n, n, j, 4 * n + 2 * b + j)
        return c

    lax.fori_loop(0, PEERS, one_peer, 0, unroll=8)
    send.wait()


GROUP = 128


def grid_kernel(
    ints_in, i_ref, own_ref, other_ref, taper_in, rep_in, col_in, row_in, out_ref,
    ints_ref, taper_ref, rep_ref, col_ref, row_ref, acc_ref, sem,
):
    pairs = (
        (ints_in, ints_ref), (taper_in, taper_ref), (rep_in, rep_ref), (col_in, col_ref), (row_in, row_ref),
    )
    copies = fetch(pairs, sem)
    core = lax.axis_index("core")
    acc_ref[...] = jnp.zeros(acc_ref.shape, F32)
    for copy in copies:
        copy.wait()
    taper = taper_ref[...]
    lane = lax.broadcasted_iota(jnp.int32, (8, 128), 1)
    sub = lax.broadcasted_iota(jnp.int32, (8, 128), 0)
    cell = lane % 32
    lane16 = lax.broadcasted_iota(jnp.int32, (16, 128), 1) // 32
    upper = lax.broadcasted_iota(jnp.int32, (16, 128), 0) // 8
    group_mask = [(lane16 == 2 * a + upper).astype(F32).astype(BF16) for a in range(2)]

    def station(z_core, at):
        where = ((at >> 3) * 8 + (z_core >> 1)) * 8 + (at & 7)
        mine = (z_core & 1) == core
        return jnp.where(mine, own_ref[where], other_ref[where]).astype(F32)

    def place(g, k):
        return g * GROUP + k

    def one_group(g, c):
        lhs_re, lhs_im = [], []
        for k in range(GROUP):
            at = place(g, k)
            sp = station(ints_ref[0, at], ints_ref[1, at])
            sq = station(ints_ref[2, at], ints_ref[3, at])
            pr, pi, qr, qi = sp[:8], sp[8:], sq[:8], sq[8:]
            gain_re = (pr * qr + pi * qi) * taper
            gain_im = (pr * qi - pi * qr) * taper
            twice_re = jnp.concatenate([gain_re, gain_re], 0).astype(BF16)
            twice_im = jnp.concatenate([gain_im, gain_im], 0).astype(BF16)
            lhs_re += [twice_re * m for m in group_mask]
            lhs_im += [twice_im * m for m in group_mask]
        wide_re = jnp.dot(jnp.concatenate(lhs_re, 0), rep_ref[0], preferred_element_type=F32)
        wide_im = jnp.dot(jnp.concatenate(lhs_im, 0), rep_ref[1], preferred_element_type=F32)
        image = i_ref[pl.ds(g * GROUP, GROUP)].reshape(GROUP * SUB, 128)
        swapped = pltpu.roll(image, 64, 1)
        corrected = (wide_re * image + wide_im * swapped).astype(BF16)
        half = jnp.dot(corrected, col_ref[...], preferred_element_type=F32).astype(BF16)
        stacked = jnp.concatenate(
            [
                jnp.concatenate([half[k * 32 : k * 32 + 32, :128], half[k * 32 : k * 32 + 32, 128:]], axis=0)
                for k in range(GROUP)
            ],
            axis=1,
        )
        cells = jnp.dot(row_ref[...], stacked, preferred_element_type=F32)
        for k in range(GROUP):
            at = place(g, k)
            row8, row_shift = ints_ref[4, at], ints_ref[5, at]
            col32, col_shift = ints_ref[6, at], ints_ref[7, at]
            keep_col = cell >= col_shift
            keep_row = sub >= row_shift
            for part in range(4):
                s = cells[part * 8 : part * 8 + 8, k * 128 : k * 128 + 128]
                near = jnp.where(keep_col, s, 0.0)
                far = s - near
                for piece, block in ((near, col32), (far, col32 + 1)):
                    if part == 0:
                        top = jnp.where(keep_row, piece, 0.0)
                        acc_ref[block, row8] += top
                        acc_ref[block, row8 + 4] += piece - top
                    else:
                        acc_ref[block, row8 + part] += piece
        return c

    lax.fori_loop(0, 2 * SLOTS // GROUP, one_group, 0)
    for band in range(16):
        for a in range(8):
            piece = acc_ref[a, 2 * band : 2 * band + 2].reshape(16, 128)
            out_ref[band, a * 16 : a * 16 + 16, :] = piece.astype(BF16)


def sum_kernel(in_ref, out_ref):
    lane = lax.broadcasted_iota(jnp.int32, (16, 128), 1) // 32
    masks = [lane == a for a in range(4)]
    for core in range(2):
        for h in range(2):
            parts = []
            for a in range(4):
                at = (h * 4 + a) * 16
                total = in_ref[core, at : at + 16, :].astype(F32)
                for z in range(1, 8):
                    total = total + in_ref[2 * z + core, at : at + 16, :].astype(F32)
                parts.append(total)
            for g in range(4):
                row = jnp.zeros((16, 128), F32)
                for a in range(4):
                    shift = (32 * (a - g)) % 128
                    moved = pltpu.roll(parts[a], shift, 1) if shift else parts[a]
                    row = jnp.where(masks[a], moved, row)
                out_ref[0, (g // 2) * 4 + 2 * core + g % 2, :, 128 * h : 128 * h + 128] = row


VM = pl.BlockSpec(memory_space=pltpu.VMEM)
SM = pl.BlockSpec(memory_space=pltpu.SMEM)
HBM = pl.BlockSpec(memory_space=pltpu.HBM)
call = functools.partial(
    pl.pallas_call, compiler_params=pltpu.CompilerParams(vmem_limit_bytes=16 << 20)
)


def pinned(x):
    return pltpu.with_memory_space_constraint(x, pltpu.HBM)


def pack(*args):
    return call(
        pack_kernel,
        out_shape=(
            jax.ShapeDtypeStruct((PEERS, 24, 256), BF16),
            jax.ShapeDtypeStruct((8, 16, 128), BF16),
        ),
        in_specs=[HBM] * 7,
        out_specs=(VM, VM),
        scratch_shapes=[pltpu.SMEM(args[0].shape, jnp.int32)]
        + [pltpu.VMEM(a.shape, a.dtype) for a in args[1:6]]
        + [
            pltpu.VMEM((8, 16, 128), BF16),
            pltpu.VMEM((32, 256), F32),
            pltpu.VMEM((128, 128), F32),
            pltpu.SMEM((SLOTS,), jnp.int32),
            pltpu.SMEM((PEERS,), jnp.int32),
            pltpu.SemaphoreType.DMA((8,)),
        ],
        name="pack",
    )(*[pinned(a) for a in args])


def collect(quarter):
    return call(
        collect_kernel,
        out_shape=jax.ShapeDtypeStruct((4, 8, 8, 16, 128), BF16),
        in_specs=[VM],
        out_specs=VM,
        name="collect",
    )(quarter)


def images(recv, sibling, freq):
    xrow = np.broadcast_to(((ROW_L - 16.0) / SUB)[:, None], (SUB, 256)).astype(np.float32)
    ycol = np.broadcast_to(((np.arange(16) + 0.5) / SUB)[:, None], (16, 256)).astype(np.float32)
    args = (freq, jnp.asarray(spread_tables(), BF16), jnp.asarray(xrow), jnp.asarray(ycol))
    return call(
        image_kernel,
        out_shape=(
            jax.ShapeDtypeStruct((2 * SLOTS, SUB, 128), F32),
            jax.ShapeDtypeStruct((8, 2 * SLOTS), jnp.int32),
        ),
        in_specs=[VM, VM] + [HBM] * 4,
        out_specs=(VM, HBM),
        scratch_shapes=[pltpu.VMEM(a.shape, a.dtype) for a in args]
        + [pltpu.VMEM((8, 2 * SLOTS), jnp.int32)]
        + [pltpu.VMEM((2 * PEERS, 8, 256), F32)] * 3
        + [pltpu.SemaphoreType.DMA((5,))],
        name="images",
    )(recv, sibling, *[pinned(a) for a in args])


def grid_tile(ints, image, own, other):
    tables = (
        jnp.asarray(taper_table()),
        jnp.asarray(replicate_tables(), BF16),
        jnp.asarray(column_table(), BF16),
        jnp.asarray(row_table(), BF16),
    )
    return call(
        grid_kernel,
        out_shape=jax.ShapeDtypeStruct((16, 128, 128), BF16),
        in_specs=[HBM, VM, VM, VM] + [HBM] * 4,
        out_specs=VM,
        scratch_shapes=[pltpu.SMEM(ints.shape, jnp.int32)]
        + [pltpu.VMEM(t.shape, t.dtype) for t in tables]
        + [pltpu.VMEM((9, 33, 8, 128), F32), pltpu.SemaphoreType.DMA((5,))],
        name="grid_tile",
    )(pinned(ints), image, own, other, *[pinned(t) for t in tables])


def band_sum(arrived):
    return call(
        sum_kernel,
        out_shape=jax.ShapeDtypeStruct((1, 8, 16, 256), F32),
        in_specs=[VM],
        out_specs=VM,
        name="band_sum",
    )(arrived)


SWAP = [(0, 1), (1, 0)]


def on_device(visibilities, weights, uv_coords, freq_ratio, screens, stations, offsets, tile_ids):
    uv = jnp.transpose(uv_coords, (1, 2, 0)).reshape(32, 32)
    pairs = jnp.transpose(screens.reshape(32, 2, 8, 128), (0, 2, 1, 3)).reshape(32, 16, 128)
    packed, mine = pack(tile_ids.T, visibilities, weights, uv, stations.T, offsets.T, pairs)
    recv = lax.all_to_all(packed, ("xh", "xl", "yh", "yl"), split_axis=0, concat_axis=0, tiled=True)
    quarter = lax.all_gather(mine, ("z", "core"), axis=0, tiled=True).reshape(8, 2, 8, 16, 128)
    own = lax.all_to_all(collect(quarter), ("xl", "yl"), split_axis=0, concat_axis=0, tiled=True).reshape(256, 16, 128)
    sibling = lax.ppermute(recv, "core", SWAP)
    image, ints = images(recv.reshape(96, 8, 256), sibling.reshape(96, 8, 256), freq_ratio[None, :])
    own, image = lax.optimization_barrier((own, image))
    other = lax.ppermute(own, "core", SWAP)
    partial = grid_tile(ints, image, own, other)
    arrived = lax.all_to_all(partial, ("z", "core"), split_axis=0, concat_axis=0, tiled=True)
    return band_sum(arrived)


def solution(mesh):
    stat, tile = mesh.shape["stat"], mesh.shape["tile"]
    every = ("z", "core", "xh", "xl", "yh", "yl")
    fine = Mesh(mesh.devices.reshape(stat // 2, 2, 2, 2, tile // 8, 2), every)
    placed = (
        P(every, None, None),
        P(every, None),
        P(every, None, None),
        P(),
        P(("z", "core"), None, None),
        P(every, None),
        P(every, None),
        P(every, None),
    )
    return jax.shard_map(
        on_device,
        mesh=fine,
        in_specs=placed,
        out_specs=P(("xh", "xl", "yh", "yl"), None, ("z", "core"), None),
        check_vma=False,
    )
```

```python
import functools
import math

import jax
import jax.numpy as jnp
import numpy as np
from jax import lax
from jax.experimental import pallas as pl
from jax.experimental.pallas import tpu as pltpu
from jax.sharding import Mesh, PartitionSpec as P

SUB = 32
TS = 256
K = 256
SLOTS = 64
PEERS = 32
F32 = jnp.float32
BF16 = jnp.bfloat16

ROW_L = np.array([4 * (r % 8) + r // 8 for r in range(SUB)])
LANE = np.arange(128)
LANE_I = LANE % 16
LANE_P = (LANE // 16) % 2
LANE_RI = LANE // 64
LANE_M = np.where((LANE // 32) % 2 == 0, 16 + LANE_I, 15 - LANE_I)


def spread_tables():
    out = np.zeros((4, 256, 256), np.float32)
    for part in range(3):
        for t in range(16):
            out[0, part * 32 + t, t * 16 : (t + 1) * 16] = 1.0
            out[1, part * 32 + 16 + t, t * 16 : (t + 1) * 16] = 1.0
    out[2, 101, :] = 1.0
    out[3, 103, :] = 1.0
    return out


def replicate_tables():
    cell = np.arange(128) % 32
    rep = (cell[:, None] == LANE_M[None, :]).astype(np.float32)
    sign = np.where(LANE_RI == 0, -1.0, 1.0).astype(np.float32)
    return np.stack([rep, rep * sign[None, :]])


def column_table():
    n = np.arange(256)
    twice, ri, p, v = n // 128, (n // 64) % 2, (n // 32) % 2, n % 32
    turns = -(LANE_M[:, None] - 16.0) * (v[None, :] - 16.0) / SUB
    turns = turns + 0.25 * (twice[None, :] - ri[None, :] + LANE_RI[:, None])
    val = np.cos(2.0 * np.pi * turns)
    return np.where(LANE_P[:, None] == p[None, :], val, 0.0)


def row_table():
    u, part, l = np.arange(32), np.arange(64) // 32, ROW_L[np.arange(64) % 32]
    angle = -2.0 * np.pi / SUB * (u[:, None] - 16.0) * (l[None, :] - 16.0)
    return np.where(part[None, :] == 0, np.cos(angle), np.sin(angle))


def taper_table():
    flat = np.arange(1024)
    l, m = flat // 32, flat % 32
    one = np.sin(np.pi * (np.arange(SUB) + 0.5) / SUB)
    return (one[l] * one[m] / (K * SUB)).reshape(8, 128).astype(np.float32)


def fit_turns():
    s = (0.5 * np.cos(np.pi * (np.arange(400) + 0.5) / 800)) ** 2
    r = np.sqrt(s)
    cheb = np.polynomial.chebyshev.Chebyshev.fit
    cos = cheb(s, np.cos(2 * np.pi * r), 5, domain=[0, 0.25]).convert(kind=np.polynomial.Polynomial)
    sin = cheb(s, np.sin(2 * np.pi * r) / r, 5, domain=[0, 0.25]).convert(kind=np.polynomial.Polynomial)
    return [float(c) for c in cos.coef], [float(c) for c in sin.coef]


COS_C, SIN_C = fit_turns()


def horner(coef, s):
    acc = jnp.full_like(s, coef[-1])
    for c in coef[-2::-1]:
        acc = acc * s + c
    return acc


def cos_sin_turns(turns):
    r = turns - jnp.round(turns)
    s = r * r
    return horner(COS_C, s), horner(SIN_C, s) * r


def fetch(pairs, sem):
    copies = [pltpu.make_async_copy(src, dst, sem.at[i]) for i, (src, dst) in enumerate(pairs)]
    for copy in copies:
        copy.start()
    return copies


def pack_kernel(
    tile_in, vis_in, weight_in, uv_in, station_in, offset_in, screen_in, out_ref, mine_ref,
    tile_ref, vis_ref, weight_ref, uv_ref, station_ref, offset_ref, screen_ref,
    meta_ref, wide_ref, src_ref, count_ref, sem,
):
    pairs = (
        (tile_in, tile_ref), (station_in, station_ref), (offset_in, offset_ref),
        (uv_in, uv_ref), (weight_in, weight_ref), (vis_in, vis_ref), (screen_in.at[pl.ds(8 * (2 * lax.axis_index("xl") + lax.axis_index("yl")), 8)], screen_ref),
    )
    copies = fetch(pairs, sem)

    def clear(i, c):
        src_ref[2 * i] = -1
        src_ref[2 * i + 1] = -1
        count_ref[i] = 0
        return c

    lax.fori_loop(0, PEERS, clear, 0, unroll=8)

    copies[0].wait()

    def assign(s, c):
        t = tile_ref[0, s]
        before = count_ref[t]
        src_ref[2 * t + before] = s
        count_ref[t] = before + 1
        return c

    lax.fori_loop(0, 32, assign, 0, unroll=4)
    for copy in copies[1:4]:
        copy.wait()
    uv = uv_ref[...]
    hi = uv.astype(BF16)
    rest = uv - hi.astype(F32)
    mid = rest.astype(BF16)
    low = (rest - mid.astype(F32)).astype(BF16)
    p, q = station_ref[0:1, :], station_ref[1:2, :]
    r, c = offset_ref[0:1, :], offset_ref[1:2, :]
    ints = jnp.concatenate([p >> 5, p & 31, q >> 5, q & 31, r >> 3, r & 7, c >> 5, c & 31], axis=0)
    columns = jnp.concatenate([hi.astype(F32), mid.astype(F32), low.astype(F32), ints.astype(F32)], axis=0)
    eye = lax.broadcasted_iota(jnp.int32, (104, 256), 0) == lax.broadcasted_iota(jnp.int32, (104, 256), 1)
    meta_ref[...] = lax.dot_general(
        columns.astype(BF16),
        eye.astype(F32).astype(BF16),
        (((0,), (0,)), ((), ())),
        preferred_element_type=F32,
    )

    row = lax.broadcasted_iota(jnp.int32, (8, 256), 0)
    for copy in copies[4:6]:
        copy.wait()

    def one_peer(n, c):
        low, high = [], []
        meta = jnp.zeros((8, 256), F32)
        for j in range(2):
            s = src_ref[2 * n + j]
            valid = s >= 0
            at = jnp.maximum(s, 0)
            weighted = jnp.where(valid, vis_ref[at] * weight_ref[pl.ds(at, 1), :], 0.0)
            low += [weighted[0:2], weighted[4:6]]
            high += [weighted[2:4], weighted[6:8]]
            meta = jnp.where(jnp.logical_and(row == j, valid), meta_ref[pl.ds(at, 1), :], meta)
        out_ref[n] = jnp.concatenate(low + high + [meta], axis=0).astype(BF16)
        return c

    lax.fori_loop(0, PEERS, one_peer, 0, unroll=16)
    copies[6].wait()
    wide_ref[...] = screen_ref[...].astype(F32).reshape(128, 128)
    parts = [wide_ref[pl.ds(ri, 64, stride=2), :].reshape(8, 8, 128) for ri in range(2)]
    mine_ref[...] = jnp.concatenate(parts, axis=1).astype(BF16)


def collect_kernel(in_ref, out_ref):
    core = lax.axis_index("core")
    for z in range(8):
        piece = in_ref[z, core]
        for x in range(4):
            out_ref[x, z] = piece


def image_kernel(
    recv_ref, other_ref, freq_in, spread_in, xrow_in, ycol_in, i_ref, ints_out,
    freq_ref, spread_ref, xrow_ref, ycol_ref, ints_ref, meta_ref, du_ref, dv_ref, sem,
):
    pairs = ((freq_in, freq_ref), (spread_in, spread_ref), (xrow_in, xrow_ref), (ycol_in, ycol_ref))
    copies = fetch(pairs, sem)
    core = lax.axis_index("core")
    for b, block_ref in enumerate((recv_ref, other_ref)):
        for n in range(PEERS):
            meta_ref[b * PEERS + n] = block_ref[3 * n + 2].astype(F32)
    meta = meta_ref[...].reshape(512, 256).astype(BF16)
    for copy in copies:
        copy.wait()
    pick16 = lax.broadcasted_iota(jnp.int32, (16, 256), 1) % 16 == lax.broadcasted_iota(jnp.int32, (16, 256), 0)
    freq = jnp.dot(
        jnp.broadcast_to(freq_ref[...], (8, 16)),
        pick16.astype(F32),
        precision=lax.Precision.HIGHEST,
        preferred_element_type=F32,
    )[0:1]
    pick = lax.broadcasted_iota(jnp.int32, (8, 256), 0) + 96 == lax.broadcasted_iota(jnp.int32, (8, 256), 1)
    ints = lax.dot_general(
        pick.astype(F32).astype(BF16), meta, (((1,), (1,)), ((), ())), preferred_element_type=F32
    )
    row = lax.broadcasted_iota(jnp.int32, (512, 128), 0)
    slot = jnp.where(row & 7 < 2, ((row >> 3) & 31) * 4 + (row >> 8) * 2 + (row & 7), -1)
    chosen = (slot == lax.broadcasted_iota(jnp.int32, (512, 128), 1)).astype(F32).astype(BF16)
    ints_ref[...] = jnp.dot(ints.astype(BF16), chosen, preferred_element_type=F32).astype(jnp.int32)
    send = pltpu.make_async_copy(ints_ref, ints_out, sem.at[4])
    send.start()

    def spread(k):
        return jnp.dot(meta, spread_ref[k], preferred_element_type=F32)

    du_ref[...] = (spread(0) * freq + spread(2)).reshape(2 * PEERS, 8, 256)
    dv_ref[...] = (spread(1) * freq + spread(3)).reshape(2 * PEERS, 8, 256)

    def one_slot(block_ref, row, n, j, slot):
        du = du_ref[row, j : j + 1, :]
        dv = dv_ref[row, j : j + 1, :]
        cu, su = cos_sin_turns(xrow_ref[...] * du - dv * (0.5 / SUB))
        cv, sv = cos_sin_turns(ycol_ref[...] * dv)
        left = jnp.concatenate([cu.astype(BF16), su.astype(BF16)], axis=1)
        w = block_ref[3 * n + core].astype(F32)[4 * j : 4 * j + 4, :]
        table = {}
        for p in range(2):
            re, im = w[p : p + 1, :], w[2 + p : 3 + p, :]
            for ri, (a, b) in enumerate(((re * cv, im * sv), (im * cv, re * sv))):
                minus, plus = (a - b).astype(BF16), (a + b).astype(BF16)
                table[ri, 0, p] = minus if ri == 0 else plus
                table[ri, 1, p] = plus if ri == 0 else minus
        keys = [(ri, s, p) for ri in range(2) for s in range(2) for p in range(2)]
        direct = jnp.concatenate([table[key] for key in keys], axis=0)
        turned = jnp.concatenate([-table[1, s, p] if ri == 0 else table[0, s, p] for ri, s, p in keys], axis=0)
        right = jnp.concatenate([direct, turned], axis=1)
        i_ref[slot] = lax.dot_general(left, right, (((1,), (1,)), ((), ())), preferred_element_type=F32)

    def one_peer(n, c):
        for b, block_ref in enumerate((recv_ref, other_ref)):
            for j in range(2):
                one_slot(block_ref, b * PEERS + n, n, j, 4 * n + 2 * b + j)
        return c

    lax.fori_loop(0, PEERS, one_peer, 0, unroll=8)
    send.wait()


GROUP = 128


def grid_kernel(
    ints_in, i_ref, own_ref, other_ref, taper_in, rep_in, col_in, row_in, out_ref,
    ints_ref, taper_ref, rep_ref, col_ref, row_ref, acc_ref, sem,
):
    pairs = (
        (ints_in, ints_ref), (taper_in, taper_ref), (rep_in, rep_ref), (col_in, col_ref), (row_in, row_ref),
    )
    copies = fetch(pairs, sem)
    core = lax.axis_index("core")
    acc_ref[...] = jnp.zeros(acc_ref.shape, F32)
    for copy in copies:
        copy.wait()
    taper = taper_ref[...]
    lane = lax.broadcasted_iota(jnp.int32, (8, 128), 1)
    sub = lax.broadcasted_iota(jnp.int32, (8, 128), 0)
    cell = lane % 32
    lane16 = lax.broadcasted_iota(jnp.int32, (16, 128), 1) // 32
    upper = lax.broadcasted_iota(jnp.int32, (16, 128), 0) // 8
    group_mask = [(lane16 == 2 * a + upper).astype(F32).astype(BF16) for a in range(2)]

    def station(z_core, at):
        where = ((at >> 3) * 8 + (z_core >> 1)) * 8 + (at & 7)
        mine = (z_core & 1) == core
        return jnp.where(mine, own_ref[where], other_ref[where]).astype(F32)

    def place(g, k):
        return g * GROUP + k

    def one_group(g, c):
        lhs_re, lhs_im = [], []
        for k in range(GROUP):
            at = place(g, k)
            sp = station(ints_ref[0, at], ints_ref[1, at])
            sq = station(ints_ref[2, at], ints_ref[3, at])
            pr, pi, qr, qi = sp[:8], sp[8:], sq[:8], sq[8:]
            gain_re = (pr * qr + pi * qi) * taper
            gain_im = (pr * qi - pi * qr) * taper
            twice_re = jnp.concatenate([gain_re, gain_re], 0).astype(BF16)
            twice_im = jnp.concatenate([gain_im, gain_im], 0).astype(BF16)
            lhs_re += [twice_re * m for m in group_mask]
            lhs_im += [twice_im * m for m in group_mask]
        wide_re = jnp.dot(jnp.concatenate(lhs_re, 0), rep_ref[0], preferred_element_type=F32)
        wide_im = jnp.dot(jnp.concatenate(lhs_im, 0), rep_ref[1], preferred_element_type=F32)
        image = i_ref[pl.ds(g * GROUP, GROUP)].reshape(GROUP * SUB, 128)
        swapped = pltpu.roll(image, 64, 1)
        corrected = (wide_re * image + wide_im * swapped).astype(BF16)
        half = jnp.dot(corrected, col_ref[...], preferred_element_type=F32).astype(BF16)
        stacked = jnp.concatenate(
            [
                jnp.concatenate([half[k * 32 : k * 32 + 32, :128], half[k * 32 : k * 32 + 32, 128:]], axis=0)
                for k in range(GROUP)
            ],
            axis=1,
        )
        cells = jnp.dot(row_ref[...], stacked, preferred_element_type=F32)
        for k in range(GROUP):
            at = place(g, k)
            row8, row_shift = ints_ref[4, at], ints_ref[5, at]
            col32, col_shift = ints_ref[6, at], ints_ref[7, at]
            keep_col = cell >= col_shift
            keep_row = sub >= row_shift
            for part in range(4):
                s = cells[part * 8 : part * 8 + 8, k * 128 : k * 128 + 128]
                near = jnp.where(keep_col, s, 0.0)
                far = s - near
                for piece, block in ((near, col32), (far, col32 + 1)):
                    if part == 0:
                        top = jnp.where(keep_row, piece, 0.0)
                        acc_ref[block, row8] += top
                        acc_ref[block, row8 + 4] += piece - top
                    else:
                        acc_ref[block, row8 + part] += piece
        return c

    lax.fori_loop(0, 2 * SLOTS // GROUP, one_group, 0)
    for band in range(16):
        for a in range(8):
            piece = acc_ref[a, 2 * band : 2 * band + 2].reshape(16, 128)
            out_ref[(band % 2) * 8 + band // 2, a * 16 : a * 16 + 16, :] = piece.astype(BF16)


def sum_kernel(in_ref, out_ref):
    lane = lax.broadcasted_iota(jnp.int32, (16, 128), 1) // 32
    masks = [lane == a for a in range(4)]
    for core in range(2):
        for h in range(2):
            parts = []
            for a in range(4):
                at = (h * 4 + a) * 16
                total = in_ref[8 * core, at : at + 16, :].astype(F32)
                for z in range(1, 8):
                    total = total + in_ref[8 * core + z, at : at + 16, :].astype(F32)
                parts.append(total)
            for g in range(4):
                row = jnp.zeros((16, 128), F32)
                for a in range(4):
                    shift = (32 * (a - g)) % 128
                    moved = pltpu.roll(parts[a], shift, 1) if shift else parts[a]
                    row = jnp.where(masks[a], moved, row)
                out_ref[0, (g // 2) * 4 + 2 * core + g % 2, :, 128 * h : 128 * h + 128] = row


VM = pl.BlockSpec(memory_space=pltpu.VMEM)
SM = pl.BlockSpec(memory_space=pltpu.SMEM)
HBM = pl.BlockSpec(memory_space=pltpu.HBM)
call = functools.partial(
    pl.pallas_call, compiler_params=pltpu.CompilerParams(vmem_limit_bytes=16 << 20)
)


def pinned(x):
    return pltpu.with_memory_space_constraint(x, pltpu.HBM)


def pack(*args):
    return call(
        pack_kernel,
        out_shape=(
            jax.ShapeDtypeStruct((PEERS, 24, 256), BF16),
            jax.ShapeDtypeStruct((8, 16, 128), BF16),
        ),
        in_specs=[HBM] * 7,
        out_specs=(VM, VM),
        scratch_shapes=[pltpu.SMEM(args[0].shape, jnp.int32)]
        + [pltpu.VMEM(a.shape, a.dtype) for a in args[1:6]]
        + [
            pltpu.VMEM((8, 16, 128), BF16),
            pltpu.VMEM((32, 256), F32),
            pltpu.VMEM((128, 128), F32),
            pltpu.SMEM((SLOTS,), jnp.int32),
            pltpu.SMEM((PEERS,), jnp.int32),
            pltpu.SemaphoreType.DMA((8,)),
        ],
        name="pack",
    )(*[pinned(a) for a in args])


def collect(quarter):
    return call(
        collect_kernel,
        out_shape=jax.ShapeDtypeStruct((4, 8, 8, 16, 128), BF16),
        in_specs=[VM],
        out_specs=VM,
        name="collect",
    )(quarter)


def images(recv, sibling, freq):
    xrow = np.broadcast_to(((ROW_L - 16.0) / SUB)[:, None], (SUB, 256)).astype(np.float32)
    ycol = np.broadcast_to(((np.arange(16) + 0.5) / SUB)[:, None], (16, 256)).astype(np.float32)
    args = (freq, jnp.asarray(spread_tables(), BF16), jnp.asarray(xrow), jnp.asarray(ycol))
    return call(
        image_kernel,
        out_shape=(
            jax.ShapeDtypeStruct((2 * SLOTS, SUB, 128), F32),
            jax.ShapeDtypeStruct((8, 2 * SLOTS), jnp.int32),
        ),
        in_specs=[VM, VM] + [HBM] * 4,
        out_specs=(VM, HBM),
        scratch_shapes=[pltpu.VMEM(a.shape, a.dtype) for a in args]
        + [pltpu.VMEM((8, 2 * SLOTS), jnp.int32)]
        + [pltpu.VMEM((2 * PEERS, 8, 256), F32)] * 3
        + [pltpu.SemaphoreType.DMA((5,))],
        name="images",
    )(recv, sibling, *[pinned(a) for a in args])


def grid_tile(ints, image, own, other):
    tables = (
        jnp.asarray(taper_table()),
        jnp.asarray(replicate_tables(), BF16),
        jnp.asarray(column_table(), BF16),
        jnp.asarray(row_table(), BF16),
    )
    return call(
        grid_kernel,
        out_shape=jax.ShapeDtypeStruct((16, 128, 128), BF16),
        in_specs=[HBM, VM, VM, VM] + [HBM] * 4,
        out_specs=VM,
        scratch_shapes=[pltpu.SMEM(ints.shape, jnp.int32)]
        + [pltpu.VMEM(t.shape, t.dtype) for t in tables]
        + [pltpu.VMEM((9, 33, 8, 128), F32), pltpu.SemaphoreType.DMA((5,))],
        name="grid_tile",
    )(pinned(ints), image, own, other, *[pinned(t) for t in tables])


def band_sum(arrived):
    return call(
        sum_kernel,
        out_shape=jax.ShapeDtypeStruct((1, 8, 16, 256), F32),
        in_specs=[VM],
        out_specs=VM,
        name="band_sum",
    )(arrived)


SWAP = [(0, 1), (1, 0)]


def on_device(visibilities, weights, uv_coords, freq_ratio, screens, stations, offsets, tile_ids):
    uv = jnp.transpose(uv_coords, (1, 2, 0)).reshape(32, 32)
    pairs = jnp.transpose(screens.reshape(32, 2, 8, 128), (0, 2, 1, 3)).reshape(32, 16, 128)
    packed, mine = pack(tile_ids.T, visibilities, weights, uv, stations.T, offsets.T, pairs)
    recv = lax.all_to_all(packed, ("xh", "xl", "yh", "yl"), split_axis=0, concat_axis=0, tiled=True)
    quarter = lax.all_gather(mine, ("z", "core"), axis=0, tiled=True).reshape(8, 2, 8, 16, 128)
    own = lax.all_to_all(collect(quarter), ("xl", "yl"), split_axis=0, concat_axis=0, tiled=True).reshape(256, 16, 128)
    sibling = lax.ppermute(recv, "core", SWAP)
    image, ints = images(recv.reshape(96, 8, 256), sibling.reshape(96, 8, 256), freq_ratio[None, :])
    own, image = lax.optimization_barrier((own, image))
    other = lax.ppermute(own, "core", SWAP)
    partial = grid_tile(ints, image, own, other)
    arrived = lax.all_to_all(partial, ("core", "z"), split_axis=0, concat_axis=0, tiled=True)
    return band_sum(arrived)


def solution(mesh):
    stat, tile = mesh.shape["stat"], mesh.shape["tile"]
    every = ("z", "core", "xh", "xl", "yh", "yl")
    fine = Mesh(mesh.devices.reshape(stat // 2, 2, 2, 2, tile // 8, 2), every)
    placed = (
        P(every, None, None),
        P(every, None),
        P(every, None, None),
        P(),
        P(("z", "core"), None, None),
        P(every, None),
        P(every, None),
        P(every, None),
    )
    return jax.shard_map(
        on_device,
        mesh=fine,
        in_specs=placed,
        out_specs=P(("xh", "xl", "yh", "yl"), None, ("z", "core"), None),
        check_vma=False,
    )
```

```python
import functools
import math

import jax
import jax.numpy as jnp
import numpy as np
from jax import lax
from jax.experimental import pallas as pl
from jax.experimental.pallas import tpu as pltpu
from jax.sharding import Mesh, PartitionSpec as P

SUB = 32
TS = 256
K = 256
SLOTS = 64
PEERS = 32
F32 = jnp.float32
BF16 = jnp.bfloat16

ROW_L = np.array([4 * (r % 8) + r // 8 for r in range(SUB)])
LANE = np.arange(128)
LANE_I = LANE % 16
LANE_P = (LANE // 16) % 2
LANE_RI = LANE // 64
LANE_M = np.where((LANE // 32) % 2 == 0, 16 + LANE_I, 15 - LANE_I)


def spread_tables():
    out = np.zeros((4, 256, 256), np.float32)
    for part in range(3):
        for t in range(16):
            out[0, part * 32 + t, t * 16 : (t + 1) * 16] = 1.0
            out[1, part * 32 + 16 + t, t * 16 : (t + 1) * 16] = 1.0
    out[2, 101, :] = 1.0
    out[3, 103, :] = 1.0
    return out


def replicate_tables():
    cell = np.arange(128) % 32
    rep = (cell[:, None] == LANE_M[None, :]).astype(np.float32)
    sign = np.where(LANE_RI == 0, -1.0, 1.0).astype(np.float32)
    return np.stack([rep, rep * sign[None, :]])


def column_table():
    n = np.arange(256)
    twice, ri, p, v = n // 128, (n // 64) % 2, (n // 32) % 2, n % 32
    turns = -(LANE_M[:, None] - 16.0) * (v[None, :] - 16.0) / SUB
    turns = turns + 0.25 * (twice[None, :] - ri[None, :] + LANE_RI[:, None])
    val = np.cos(2.0 * np.pi * turns)
    return np.where(LANE_P[:, None] == p[None, :], val, 0.0)


def row_table():
    u, part, l = np.arange(32), np.arange(64) // 32, ROW_L[np.arange(64) % 32]
    angle = -2.0 * np.pi / SUB * (u[:, None] - 16.0) * (l[None, :] - 16.0)
    return np.where(part[None, :] == 0, np.cos(angle), np.sin(angle))


def taper_table():
    flat = np.arange(1024)
    l, m = flat // 32, flat % 32
    one = np.sin(np.pi * (np.arange(SUB) + 0.5) / SUB)
    return (one[l] * one[m] / (K * SUB)).reshape(8, 128).astype(np.float32)


def fit_turns():
    s = (0.5 * np.cos(np.pi * (np.arange(400) + 0.5) / 800)) ** 2
    r = np.sqrt(s)
    cheb = np.polynomial.chebyshev.Chebyshev.fit
    cos = cheb(s, np.cos(2 * np.pi * r), 5, domain=[0, 0.25]).convert(kind=np.polynomial.Polynomial)
    sin = cheb(s, np.sin(2 * np.pi * r) / r, 5, domain=[0, 0.25]).convert(kind=np.polynomial.Polynomial)
    return [float(c) for c in cos.coef], [float(c) for c in sin.coef]


COS_C, SIN_C = fit_turns()


def horner(coef, s):
    acc = jnp.full_like(s, coef[-1])
    for c in coef[-2::-1]:
        acc = acc * s + c
    return acc


def cos_sin_turns(turns):
    r = turns - jnp.round(turns)
    s = r * r
    return horner(COS_C, s), horner(SIN_C, s) * r


def fetch(pairs, sem):
    copies = [pltpu.make_async_copy(src, dst, sem.at[i]) for i, (src, dst) in enumerate(pairs)]
    for copy in copies:
        copy.start()
    return copies


def pack_kernel(
    tile_in, vis_in, weight_in, uv_in, station_in, offset_in, screen_in, out_ref, mine_ref,
    tile_ref, vis_ref, weight_ref, uv_ref, station_ref, offset_ref, screen_ref,
    meta_ref, wide_ref, src_ref, count_ref, sem,
):
    pairs = (
        (tile_in, tile_ref), (station_in, station_ref), (offset_in, offset_ref),
        (uv_in, uv_ref), (weight_in, weight_ref), (vis_in, vis_ref), (screen_in.at[pl.ds(8 * (2 * lax.axis_index("yl") + lax.axis_index("xl")), 8)], screen_ref),
    )
    copies = fetch(pairs, sem)

    def clear(i, c):
        src_ref[2 * i] = -1
        src_ref[2 * i + 1] = -1
        count_ref[i] = 0
        return c

    lax.fori_loop(0, PEERS, clear, 0, unroll=8)

    copies[0].wait()

    def assign(s, c):
        t = tile_ref[0, s]
        before = count_ref[t]
        src_ref[2 * t + before] = s
        count_ref[t] = before + 1
        return c

    lax.fori_loop(0, 32, assign, 0, unroll=4)
    for copy in copies[1:4]:
        copy.wait()
    uv = uv_ref[...]
    hi = uv.astype(BF16)
    rest = uv - hi.astype(F32)
    mid = rest.astype(BF16)
    low = (rest - mid.astype(F32)).astype(BF16)
    p, q = station_ref[0:1, :], station_ref[1:2, :]
    r, c = offset_ref[0:1, :], offset_ref[1:2, :]
    ints = jnp.concatenate([p >> 5, p & 31, q >> 5, q & 31, r >> 3, r & 7, c >> 5, c & 31], axis=0)
    columns = jnp.concatenate([hi.astype(F32), mid.astype(F32), low.astype(F32), ints.astype(F32)], axis=0)
    eye = lax.broadcasted_iota(jnp.int32, (104, 256), 0) == lax.broadcasted_iota(jnp.int32, (104, 256), 1)
    meta_ref[...] = lax.dot_general(
        columns.astype(BF16),
        eye.astype(F32).astype(BF16),
        (((0,), (0,)), ((), ())),
        preferred_element_type=F32,
    )

    row = lax.broadcasted_iota(jnp.int32, (8, 256), 0)
    for copy in copies[4:6]:
        copy.wait()

    def one_peer(n, c):
        low, high = [], []
        meta = jnp.zeros((8, 256), F32)
        for j in range(2):
            s = src_ref[2 * n + j]
            valid = s >= 0
            at = jnp.maximum(s, 0)
            weighted = jnp.where(valid, vis_ref[at] * weight_ref[pl.ds(at, 1), :], 0.0)
            low += [weighted[0:2], weighted[4:6]]
            high += [weighted[2:4], weighted[6:8]]
            meta = jnp.where(jnp.logical_and(row == j, valid), meta_ref[pl.ds(at, 1), :], meta)
        out_ref[n] = jnp.concatenate(low + high + [meta], axis=0).astype(BF16)
        return c

    lax.fori_loop(0, PEERS, one_peer, 0, unroll=16)
    copies[6].wait()
    wide_ref[...] = screen_ref[...].astype(F32).reshape(128, 128)
    parts = [wide_ref[pl.ds(ri, 64, stride=2), :].reshape(8, 8, 128) for ri in range(2)]
    mine_ref[...] = jnp.concatenate(parts, axis=1).astype(BF16)


def collect_kernel(in_ref, out_ref):
    core = lax.axis_index("core")
    for z in range(8):
        piece = in_ref[z, core]
        for x in range(4):
            out_ref[x, z] = piece


def image_kernel(
    recv_ref, other_ref, freq_in, spread_in, xrow_in, ycol_in, i_ref, ints_out,
    freq_ref, spread_ref, xrow_ref, ycol_ref, ints_ref, meta_ref, du_ref, dv_ref, sem,
):
    pairs = ((freq_in, freq_ref), (spread_in, spread_ref), (xrow_in, xrow_ref), (ycol_in, ycol_ref))
    copies = fetch(pairs, sem)
    core = lax.axis_index("core")
    for b, block_ref in enumerate((recv_ref, other_ref)):
        for n in range(PEERS):
            meta_ref[b * PEERS + n] = block_ref[3 * n + 2].astype(F32)
    meta = meta_ref[...].reshape(512, 256).astype(BF16)
    for copy in copies:
        copy.wait()
    pick16 = lax.broadcasted_iota(jnp.int32, (16, 256), 1) % 16 == lax.broadcasted_iota(jnp.int32, (16, 256), 0)
    freq = jnp.dot(
        jnp.broadcast_to(freq_ref[...], (8, 16)),
        pick16.astype(F32),
        precision=lax.Precision.HIGHEST,
        preferred_element_type=F32,
    )[0:1]
    pick = lax.broadcasted_iota(jnp.int32, (8, 256), 0) + 96 == lax.broadcasted_iota(jnp.int32, (8, 256), 1)
    ints = lax.dot_general(
        pick.astype(F32).astype(BF16), meta, (((1,), (1,)), ((), ())), preferred_element_type=F32
    )
    row = lax.broadcasted_iota(jnp.int32, (512, 128), 0)
    slot = jnp.where(row & 7 < 2, ((row >> 3) & 31) * 4 + (row >> 8) * 2 + (row & 7), -1)
    chosen = (slot == lax.broadcasted_iota(jnp.int32, (512, 128), 1)).astype(F32).astype(BF16)
    ints_ref[...] = jnp.dot(ints.astype(BF16), chosen, preferred_element_type=F32).astype(jnp.int32)
    send = pltpu.make_async_copy(ints_ref, ints_out, sem.at[4])
    send.start()

    def spread(k):
        return jnp.dot(meta, spread_ref[k], preferred_element_type=F32)

    du_ref[...] = (spread(0) * freq + spread(2)).reshape(2 * PEERS, 8, 256)
    dv_ref[...] = (spread(1) * freq + spread(3)).reshape(2 * PEERS, 8, 256)

    def one_slot(block_ref, row, n, j, slot):
        du = du_ref[row, j : j + 1, :]
        dv = dv_ref[row, j : j + 1, :]
        cu, su = cos_sin_turns(xrow_ref[...] * du - dv * (0.5 / SUB))
        cv, sv = cos_sin_turns(ycol_ref[...] * dv)
        left = jnp.concatenate([cu.astype(BF16), su.astype(BF16)], axis=1)
        w = block_ref[3 * n + core].astype(F32)[4 * j : 4 * j + 4, :]
        table = {}
        for p in range(2):
            re, im = w[p : p + 1, :], w[2 + p : 3 + p, :]
            for ri, (a, b) in enumerate(((re * cv, im * sv), (im * cv, re * sv))):
                minus, plus = (a - b).astype(BF16), (a + b).astype(BF16)
                table[ri, 0, p] = minus if ri == 0 else plus
                table[ri, 1, p] = plus if ri == 0 else minus
        keys = [(ri, s, p) for ri in range(2) for s in range(2) for p in range(2)]
        direct = jnp.concatenate([table[key] for key in keys], axis=0)
        turned = jnp.concatenate([-table[1, s, p] if ri == 0 else table[0, s, p] for ri, s, p in keys], axis=0)
        right = jnp.concatenate([direct, turned], axis=1)
        i_ref[slot] = lax.dot_general(left, right, (((1,), (1,)), ((), ())), preferred_element_type=F32)

    def one_peer(n, c):
        for b, block_ref in enumerate((recv_ref, other_ref)):
            for j in range(2):
                one_slot(block_ref, b * PEERS + n, n, j, 4 * n + 2 * b + j)
        return c

    lax.fori_loop(0, PEERS, one_peer, 0, unroll=8)
    send.wait()


GROUP = 128


def grid_kernel(
    ints_in, i_ref, own_ref, other_ref, taper_in, rep_in, col_in, row_in, out_ref,
    ints_ref, taper_ref, rep_ref, col_ref, row_ref, acc_ref, sem,
):
    pairs = (
        (ints_in, ints_ref), (taper_in, taper_ref), (rep_in, rep_ref), (col_in, col_ref), (row_in, row_ref),
    )
    copies = fetch(pairs, sem)
    core = lax.axis_index("core")
    acc_ref[...] = jnp.zeros(acc_ref.shape, F32)
    for copy in copies:
        copy.wait()
    taper = taper_ref[...]
    lane = lax.broadcasted_iota(jnp.int32, (8, 128), 1)
    sub = lax.broadcasted_iota(jnp.int32, (8, 128), 0)
    cell = lane % 32
    lane16 = lax.broadcasted_iota(jnp.int32, (16, 128), 1) // 32
    upper = lax.broadcasted_iota(jnp.int32, (16, 128), 0) // 8
    group_mask = [(lane16 == 2 * a + upper).astype(F32).astype(BF16) for a in range(2)]

    def station(z_core, at):
        where = ((at >> 3) * 8 + (z_core >> 1)) * 8 + (at & 7)
        mine = (z_core & 1) == core
        return jnp.where(mine, own_ref[where], other_ref[where]).astype(F32)

    def place(g, k):
        return g * GROUP + k

    def one_group(g, c):
        lhs_re, lhs_im = [], []
        for k in range(GROUP):
            at = place(g, k)
            sp = station(ints_ref[0, at], ints_ref[1, at])
            sq = station(ints_ref[2, at], ints_ref[3, at])
            pr, pi, qr, qi = sp[:8], sp[8:], sq[:8], sq[8:]
            gain_re = (pr * qr + pi * qi) * taper
            gain_im = (pr * qi - pi * qr) * taper
            twice_re = jnp.concatenate([gain_re, gain_re], 0).astype(BF16)
            twice_im = jnp.concatenate([gain_im, gain_im], 0).astype(BF16)
            lhs_re += [twice_re * m for m in group_mask]
            lhs_im += [twice_im * m for m in group_mask]
        wide_re = jnp.dot(jnp.concatenate(lhs_re, 0), rep_ref[0], preferred_element_type=F32)
        wide_im = jnp.dot(jnp.concatenate(lhs_im, 0), rep_ref[1], preferred_element_type=F32)
        image = i_ref[pl.ds(g * GROUP, GROUP)].reshape(GROUP * SUB, 128)
        swapped = pltpu.roll(image, 64, 1)
        corrected = (wide_re * image + wide_im * swapped).astype(BF16)
        half = jnp.dot(corrected, col_ref[...], preferred_element_type=F32).astype(BF16)
        stacked = jnp.concatenate(
            [
                jnp.concatenate([half[k * 32 : k * 32 + 32, :128], half[k * 32 : k * 32 + 32, 128:]], axis=0)
                for k in range(GROUP)
            ],
            axis=1,
        )
        cells = jnp.dot(row_ref[...], stacked, preferred_element_type=F32)
        for k in range(GROUP):
            at = place(g, k)
            row8, row_shift = ints_ref[4, at], ints_ref[5, at]
            col32, col_shift = ints_ref[6, at], ints_ref[7, at]
            keep_col = cell >= col_shift
            keep_row = sub >= row_shift
            for part in range(4):
                s = cells[part * 8 : part * 8 + 8, k * 128 : k * 128 + 128]
                near = jnp.where(keep_col, s, 0.0)
                far = s - near
                for piece, block in ((near, col32), (far, col32 + 1)):
                    if part == 0:
                        top = jnp.where(keep_row, piece, 0.0)
                        acc_ref[block, row8] += top
                        acc_ref[block, row8 + 4] += piece - top
                    else:
                        acc_ref[block, row8 + part] += piece
        return c

    lax.fori_loop(0, 2 * SLOTS // GROUP, one_group, 0)
    for band in range(16):
        for a in range(8):
            piece = acc_ref[a, 2 * band : 2 * band + 2].reshape(16, 128)
            out_ref[(band % 2) * 8 + band // 2, a * 16 : a * 16 + 16, :] = piece.astype(BF16)


def sum_kernel(in_ref, out_ref):
    lane = lax.broadcasted_iota(jnp.int32, (16, 128), 1) // 32
    masks = [lane == a for a in range(4)]
    for core in range(2):
        for h in range(2):
            parts = []
            for a in range(4):
                at = (h * 4 + a) * 16
                total = in_ref[8 * core, at : at + 16, :].astype(F32)
                for z in range(1, 8):
                    total = total + in_ref[8 * core + z, at : at + 16, :].astype(F32)
                parts.append(total)
            for g in range(4):
                row = jnp.zeros((16, 128), F32)
                for a in range(4):
                    shift = (32 * (a - g)) % 128
                    moved = pltpu.roll(parts[a], shift, 1) if shift else parts[a]
                    row = jnp.where(masks[a], moved, row)
                out_ref[0, (g // 2) * 4 + 2 * core + g % 2, :, 128 * h : 128 * h + 128] = row


VM = pl.BlockSpec(memory_space=pltpu.VMEM)
SM = pl.BlockSpec(memory_space=pltpu.SMEM)
HBM = pl.BlockSpec(memory_space=pltpu.HBM)
call = functools.partial(
    pl.pallas_call, compiler_params=pltpu.CompilerParams(vmem_limit_bytes=16 << 20)
)


def pinned(x):
    return pltpu.with_memory_space_constraint(x, pltpu.HBM)


def pack(*args):
    return call(
        pack_kernel,
        out_shape=(
            jax.ShapeDtypeStruct((PEERS, 24, 256), BF16),
            jax.ShapeDtypeStruct((8, 16, 128), BF16),
        ),
        in_specs=[HBM] * 7,
        out_specs=(VM, VM),
        scratch_shapes=[pltpu.SMEM(args[0].shape, jnp.int32)]
        + [pltpu.VMEM(a.shape, a.dtype) for a in args[1:6]]
        + [
            pltpu.VMEM((8, 16, 128), BF16),
            pltpu.VMEM((32, 256), F32),
            pltpu.VMEM((128, 128), F32),
            pltpu.SMEM((SLOTS,), jnp.int32),
            pltpu.SMEM((PEERS,), jnp.int32),
            pltpu.SemaphoreType.DMA((8,)),
        ],
        name="pack",
    )(*[pinned(a) for a in args])


def collect(quarter):
    return call(
        collect_kernel,
        out_shape=jax.ShapeDtypeStruct((4, 8, 8, 16, 128), BF16),
        in_specs=[VM],
        out_specs=VM,
        name="collect",
    )(quarter)


def images(recv, sibling, freq):
    xrow = np.broadcast_to(((ROW_L - 16.0) / SUB)[:, None], (SUB, 256)).astype(np.float32)
    ycol = np.broadcast_to(((np.arange(16) + 0.5) / SUB)[:, None], (16, 256)).astype(np.float32)
    args = (freq, jnp.asarray(spread_tables(), BF16), jnp.asarray(xrow), jnp.asarray(ycol))
    return call(
        image_kernel,
        out_shape=(
            jax.ShapeDtypeStruct((2 * SLOTS, SUB, 128), F32),
            jax.ShapeDtypeStruct((8, 2 * SLOTS), jnp.int32),
        ),
        in_specs=[VM, VM] + [HBM] * 4,
        out_specs=(VM, HBM),
        scratch_shapes=[pltpu.VMEM(a.shape, a.dtype) for a in args]
        + [pltpu.VMEM((8, 2 * SLOTS), jnp.int32)]
        + [pltpu.VMEM((2 * PEERS, 8, 256), F32)] * 3
        + [pltpu.SemaphoreType.DMA((5,))],
        name="images",
    )(recv, sibling, *[pinned(a) for a in args])


def grid_tile(ints, image, own, other):
    tables = (
        jnp.asarray(taper_table()),
        jnp.asarray(replicate_tables(), BF16),
        jnp.asarray(column_table(), BF16),
        jnp.asarray(row_table(), BF16),
    )
    return call(
        grid_kernel,
        out_shape=jax.ShapeDtypeStruct((16, 128, 128), BF16),
        in_specs=[HBM, VM, VM, VM] + [HBM] * 4,
        out_specs=VM,
        scratch_shapes=[pltpu.SMEM(ints.shape, jnp.int32)]
        + [pltpu.VMEM(t.shape, t.dtype) for t in tables]
        + [pltpu.VMEM((9, 33, 8, 128), F32), pltpu.SemaphoreType.DMA((5,))],
        name="grid_tile",
    )(pinned(ints), image, own, other, *[pinned(t) for t in tables])


def band_sum(arrived):
    return call(
        sum_kernel,
        out_shape=jax.ShapeDtypeStruct((1, 8, 16, 256), F32),
        in_specs=[VM],
        out_specs=VM,
        name="band_sum",
    )(arrived)


SWAP = [(0, 1), (1, 0)]


def on_device(visibilities, weights, uv_coords, freq_ratio, screens, stations, offsets, tile_ids):
    uv = jnp.transpose(uv_coords, (1, 2, 0)).reshape(32, 32)
    pairs = jnp.transpose(screens.reshape(32, 2, 8, 128), (0, 2, 1, 3)).reshape(32, 16, 128)
    packed, mine = pack(tile_ids.T, visibilities, weights, uv, stations.T, offsets.T, pairs)
    recv = lax.all_to_all(packed, ("xh", "xl", "yh", "yl"), split_axis=0, concat_axis=0, tiled=True)
    quarter = lax.all_gather(mine, ("z", "core"), axis=0, tiled=True).reshape(8, 2, 8, 16, 128)
    own = lax.all_to_all(collect(quarter), ("yl", "xl"), split_axis=0, concat_axis=0, tiled=True).reshape(256, 16, 128)
    sibling = lax.ppermute(recv, "core", SWAP)
    image, ints = images(recv.reshape(96, 8, 256), sibling.reshape(96, 8, 256), freq_ratio[None, :])
    own, image = lax.optimization_barrier((own, image))
    other = lax.ppermute(own, "core", SWAP)
    partial = grid_tile(ints, image, own, other)
    arrived = lax.all_to_all(partial, ("core", "z"), split_axis=0, concat_axis=0, tiled=True)
    return band_sum(arrived)


def solution(mesh):
    stat, tile = mesh.shape["stat"], mesh.shape["tile"]
    every = ("z", "core", "xh", "xl", "yh", "yl")
    fine = Mesh(mesh.devices.reshape(stat // 2, 2, 2, 2, tile // 8, 2), every)
    placed = (
        P(every, None, None),
        P(every, None),
        P(every, None, None),
        P(),
        P(("z", "core"), None, None),
        P(every, None),
        P(every, None),
        P(every, None),
    )
    return jax.shard_map(
        on_device,
        mesh=fine,
        in_specs=placed,
        out_specs=P(("xh", "xl", "yh", "yl"), None, ("z", "core"), None),
        check_vma=False,
    )
```
